32 devices in a mesh: segment: 4 (over z), space: 8 (over y, x, core).
Axes of the slice: x: 2, y: 2, z: 4, core: 2. Of those that a mesh axis runs over, the one named last changes fastest.
Arguments:
- text_states: bfloat16 [2, 8, 128, 4096], P(None, 'space'), may hold values from -6 to 6
- token_ids: int32 [2, 8, 128], replicated, may hold values from 0 to 32127, as said below
- step_ids: int32 [3, 2], replicated, may hold values from 100 to 899
- base_noise: bfloat16 [2, 8, 3, 1024], P(None, 'space'), may hold values from -6 to 6
- upscale_noise: bfloat16 [2, 8, 3, 1024], P(None, 'space'), may hold values from -6 to 6
- final_noise: bfloat16 [2, 8, 3, 512, 32], P(None, None, None, 'space'), may hold values from -6 to 6
- t5_gain: float32 [4096], replicated, may hold values from 0.5 to 1.5
- base_keyval: bfloat16 [4096, 1024], replicated, may hold values from -0.09375 to 0.09375
- upscale_keyval: bfloat16 [2, 4096, 256], replicated, may hold values from -0.09375 to 0.09375
- base_input: bfloat16 [3, 512], replicated, may hold values from -3.5 to 3.5
- base_time: bfloat16 [512, 512], replicated, may hold values from -0.25 to 0.25
- base_gain: float32 [3, 512], replicated, may hold values from 0.5 to 1.5
- base_conv: bfloat16 [9, 512, 512], replicated, may hold values from -0.09375 to 0.09375
- base_query: bfloat16 [512, 512], replicated, may hold values from -0.25 to 0.25
- base_output: bfloat16 [512, 512], replicated, may hold values from -0.25 to 0.25
- base_head: bfloat16 [512, 3], replicated, may hold values from -0.25 to 0.25
- upscale_input: bfloat16 [2, 6, 128], replicated, may hold values from -2.5 to 2.5
- upscale_time: bfloat16 [2, 128, 128], replicated, may hold values from -0.5 to 0.5
- upscale_gain: float32 [2, 3, 128], replicated, may hold values from 0.5 to 1.5
- upscale_conv: bfloat16 [2, 9, 128, 128], replicated, may hold values from -0.1875 to 0.1875
- upscale_query: bfloat16 [2, 128, 128], replicated, may hold values from -0.5 to 0.5
- upscale_output: bfloat16 [2, 128, 128], replicated, may hold values from -0.5 to 0.5
- upscale_head: bfloat16 [2, 128, 3], replicated, may hold values from -0.5 to 0.5
Outputs:
- early_states: bfloat16 [2, 2, 8, 3, 1024], P(None, None, 'space', None, 'segment')
- final_states: bfloat16 [2, 2, 8, 3, 512, 32], P(None, None, 'segment', None, 'space')
The draws below stay inside these ranges and needn't reach their ends.
Inputs may be any that keep to these rules, and one draw needn't show every extreme that they name: `token_ids`: each prompt's ids are nonzero on its first 1 to 128 positions and 0 (padding) after them; some prompt fills all 128 positions.
All inputs are finite; a program needn't handle non-finite values.
Results may differ from the reference program's by a relative error of at most 0.0095.
Values may be sent and summed in bfloat16 or wider, within the bound.
No kernel may reach another device: no remote copies, remote signals or barrier semaphores. Data moves between devices by JAX's collectives and lax.ppermute only.
A program may use at most 256 MiB of HBM per device.

```python
import math
import jax
import jax.numpy as jnp
from jax import lax

DT5 = 4096
VOCAB = 32128
CB = 512
CS = 128
HD = 64
LTXT = 128
SIDE = 32
ROWS2 = 512
WIN2 = 32
MICRO = 2
PX = 1024
IMGS = 8


def draw_token_ids(key, part):
    length_key = jax.random.fold_in(key, 11)
    word_key = jax.random.fold_in(key, 12)
    lengths = jax.random.randint(length_key, (MICRO, IMGS), 1, LTXT + 1)
    lengths = lengths.at[0, 0].set(LTXT)
    words = jax.random.randint(word_key, (MICRO, IMGS, LTXT), 1, VOCAB)
    position = jnp.arange(LTXT, dtype=jnp.int32)
    return jnp.where(position[None, None, :] < lengths[:, :, None], words, 0).astype(jnp.int32)


def place_ends(array, key, least, top_value):
    extent = array.shape
    index_at = [jax.random.randint(jax.random.fold_in(key, axis), (), 0, extent[axis]) for axis in range(len(extent))]
    array = array.at[tuple(index_at)].set(least)
    longest = extent.index(max(extent))
    index_at[longest] = (index_at[longest] + 1) % extent[longest]
    return array.at[tuple(index_at)].set(top_value)


def levels(key, shape, pieces, smallest, largest):
    def one(axis_at, parts):
        draws = jax.random.uniform(jax.random.fold_in(jax.random.fold_in(key, 6), axis_at), (parts,), jnp.float32, smallest / len(pieces), largest / len(pieces))
        return jnp.repeat(jnp.exp(draws), shape[axis_at] // parts).reshape((-1,) + (1,) * (len(shape) - axis_at - 1))

    level = one(*pieces[0])
    for cut in pieces[1:]:
        level = level * one(*cut)
    return level


def bell_draw(key, dims, scale, limit, shards=(), held_as=jnp.bfloat16):
    array = scale * jax.random.normal(key, dims, jnp.float32)
    if shards:
        array = array * levels(key, dims, shards, -0.22, 0.18)
    return jnp.clip(array, -limit, limit).astype(held_as)


def setup_inputs(seed: int = 0) -> dict:
    seeds = jax.random.split(jax.random.key(seed), 24)
    return {
        "text_states": bell_draw(seeds[0], (MICRO, IMGS, LTXT, DT5), 1.0, 6.0, ((1, 8),)),
        "token_ids": draw_token_ids(jax.random.fold_in(seeds[23], 71), 0),
        "step_ids": place_ends(jax.random.randint(seeds[2], (3, MICRO), 100, 900), jax.random.fold_in(seeds[2], 1), 100, 899).astype(jnp.int32),
        "base_noise": bell_draw(seeds[3], (MICRO, IMGS, 3, PX), 1.0, 6.0, ((1, 8),)),
        "upscale_noise": bell_draw(seeds[4], (MICRO, IMGS, 3, PX), 1.0, 6.0, ((1, 8),)),
        "final_noise": bell_draw(seeds[5], (MICRO, IMGS, 3, ROWS2, WIN2), 1.0, 6.0, ((3, 8),)),
        "t5_gain": jnp.clip(1.0 + 0.1 * jax.random.normal(seeds[6], (DT5,), jnp.float32), 0.5, 1.5),
        "base_keyval": bell_draw(seeds[7], (DT5, 2 * CB), DT5 ** -0.5, 0.09375),
        "upscale_keyval": bell_draw(seeds[8], (2, DT5, 2 * CS), DT5 ** -0.5, 0.09375),
        "base_input": bell_draw(seeds[9], (3, CB), 3 ** -0.5, 3.5),
        "base_time": bell_draw(seeds[10], (CB, CB), CB ** -0.5, 0.25),
        "base_gain": jnp.clip(1.0 + 0.1 * jax.random.normal(seeds[11], (3, CB), jnp.float32), 0.5, 1.5),
        "base_conv": bell_draw(seeds[12], (9, CB, CB), (9 * CB) ** -0.5, 0.09375),
        "base_query": bell_draw(seeds[13], (CB, CB), CB ** -0.5, 0.25),
        "base_output": bell_draw(seeds[14], (CB, CB), CB ** -0.5, 0.25),
        "base_head": bell_draw(seeds[15], (CB, 3), CB ** -0.5, 0.25),
        "upscale_input": bell_draw(seeds[16], (2, 6, CS), 6 ** -0.5, 2.5),
        "upscale_time": bell_draw(seeds[17], (2, CS, CS), CS ** -0.5, 0.5),
        "upscale_gain": jnp.clip(1.0 + 0.1 * jax.random.normal(seeds[18], (2, 3, CS), jnp.float32), 0.5, 1.5),
        "upscale_conv": bell_draw(seeds[19], (2, 9, CS, CS), (9 * CS) ** -0.5, 0.1875),
        "upscale_query": bell_draw(seeds[20], (2, CS, CS), CS ** -0.5, 0.5),
        "upscale_output": bell_draw(seeds[21], (2, CS, CS), CS ** -0.5, 0.5),
        "upscale_head": bell_draw(seeds[22], (2, CS, 3), CS ** -0.5, 0.5),
    }


def rms_scale(hidden, gain):
    return hidden * lax.rsqrt(lax.optimization_barrier(jnp.mean(hidden * hidden, axis=-1, keepdims=True)) + 1e-06) * gain

def alpha_bar(step):
    frac = (step.astype(jnp.float32) / 1000.0 + 0.008) / 1.008
    return jnp.cos(frac * (math.pi / 2)) ** 2

def time_embed(step, w_time):
    half = w_time.shape[0] // 2
    freqs = jnp.exp(-math.log(10000.0) * jnp.arange(half, dtype=jnp.float32) / half)
    angle = step.astype(jnp.float32) * freqs
    embed = jnp.concatenate([jnp.sin(angle), jnp.cos(angle)])[None, :].astype(jnp.bfloat16)
    return jnp.dot(embed, w_time, preferred_element_type=jnp.float32)

def pixel_rows(planes):
    return planes.reshape(planes.shape[0], -1).T

def upsample(region, height, width, rise, spread):
    grid = region.reshape(3, height, width)
    return jnp.repeat(jnp.repeat(grid, rise, axis=1), spread, axis=2)

def conv_padded(padded, w_conv):
    count = padded.shape[0]
    height = padded.shape[1] - 2
    width = padded.shape[2] - 2
    chans = padded.shape[3]
    taps = [padded[:, tap // 3:tap // 3 + height, tap % 3:tap % 3 + width, :] for tap in range(9)]
    stacked = jnp.concatenate(taps, axis=-1).reshape(count * height * width, 9 * chans)
    return jnp.dot(stacked, w_conv.reshape(9 * chans, -1), preferred_element_type=jnp.float32)

def attend(query, keyval, valid):
    count, rows, width = query.shape
    heads = width // HD
    q_four = query.astype(jnp.float32).reshape(count, rows, heads, HD)
    k_four = keyval[:, :, :width].astype(jnp.float32).reshape(count, -1, heads, HD)
    v_four = keyval[:, :, width:].astype(jnp.float32).reshape(count, -1, heads, HD)
    scores = jnp.einsum('bphd,blhd->bhpl', q_four, k_four)
    scores = jnp.where(valid[:, None, None, :], scores, -1e+30)
    weights = jax.nn.softmax(scores, axis=-1).astype(jnp.bfloat16)
    mixed = jnp.einsum('bhpl,blhd->bphd', weights.astype(jnp.float32), v_four)
    return mixed.reshape(count, rows, width).astype(jnp.bfloat16)

def front(pixels_in, step, weights):
    hidden = jnp.dot(pixels_in, weights[0], preferred_element_type=jnp.float32) + time_embed(step, weights[1])
    active = jax.nn.silu(rms_scale(hidden, weights[2][0])).astype(jnp.bfloat16)
    return (hidden, active)

def back(hidden, conv_sum, keyval, valid, noisy, step, weights):
    gains = weights[2]
    width = weights[4].shape[0]
    hidden = hidden + conv_sum
    query = jnp.dot(rms_scale(hidden, gains[1]).astype(jnp.bfloat16), weights[4], preferred_element_type=jnp.float32)
    query = (query * HD ** (-0.5)).astype(jnp.bfloat16)
    mixed = attend(query.reshape(keyval.shape[0], -1, width), keyval, valid)
    hidden = hidden + jnp.dot(mixed.reshape(-1, width), weights[5], preferred_element_type=jnp.float32)
    predicted = jnp.dot(rms_scale(hidden, gains[2]).astype(jnp.bfloat16), weights[6], preferred_element_type=jnp.float32)
    level = alpha_bar(step)
    earlier = alpha_bar(step - 50)
    clean = jnp.clip((noisy.astype(jnp.float32) - jnp.sqrt(1.0 - level) * predicted) / jnp.sqrt(level), -1.0, 1.0)
    prior = jnp.sqrt(earlier) * clean + jnp.sqrt(1.0 - earlier) * predicted
    return (clean.astype(jnp.bfloat16).T, prior.astype(jnp.bfloat16).T)

def local_section(noisy_planes, cond_planes, keyval, valid, step, weights):
    height, width = (noisy_planes.shape[1], noisy_planes.shape[2])
    planes = noisy_planes if cond_planes is None else jnp.concatenate([noisy_planes, cond_planes], axis=0)
    hidden, active = front(pixel_rows(planes), step, weights)
    padded = jnp.pad(active.reshape(1, height, width, -1), ((0, 0), (1, 1), (1, 1), (0, 0)))
    conv_sum = conv_padded(padded, weights[3])
    return back(hidden, conv_sum, keyval[None], valid[None], pixel_rows(noisy_planes), step, weights)

def project(context, weight):
    return jnp.dot(context, weight, preferred_element_type=jnp.float32).astype(jnp.bfloat16)

def reference(text_states, token_ids, step_ids, base_noise, upscale_noise, final_noise, t5_gain, base_keyval, upscale_keyval, base_input, base_time, base_gain, base_conv, base_query, base_output, base_head, upscale_input, upscale_time, upscale_gain, upscale_conv, upscale_query, upscale_output, upscale_head):
    quarter = SIDE // 4
    base_weights = (base_input, base_time, base_gain, base_conv, base_query, base_output, base_head)
    stacked = (upscale_input, upscale_time, upscale_gain, upscale_conv, upscale_query, upscale_output, upscale_head)
    first_weights = tuple((weight[0] for weight in stacked))
    last_weights = tuple((weight[1] for weight in stacked))

    def one_image(flat):
        micro = flat // IMGS
        image = flat % IMGS
        valid = token_ids[micro, image] != 0
        context = rms_scale(text_states[micro, image].astype(jnp.float32), t5_gain).astype(jnp.bfloat16)
        key_base = project(context, base_keyval)
        key_first = project(context, upscale_keyval[0])
        key_last = project(context, upscale_keyval[1])
        clean_base, prior_base = local_section(base_noise[micro, image].reshape(3, SIDE, SIDE), None, key_base, valid, step_ids[0, micro], base_weights)
        cond_first = upsample(clean_base.reshape(3, SIDE, SIDE)[:, :quarter, :quarter], quarter, quarter, 4, 4)
        clean_first, prior_first = local_section(upscale_noise[micro, image].reshape(3, SIDE, SIDE), cond_first, key_first, valid, step_ids[1, micro], first_weights)
        cond_last = upsample(clean_first, SIDE, SIDE, ROWS2 // SIDE, WIN2 // SIDE)
        clean_last, prior_last = local_section(final_noise[micro, image], cond_last, key_last, valid, step_ids[2, micro], last_weights)
        return (prior_base, prior_first, clean_last, prior_last)
    prior_base, prior_first, clean_last, prior_last = lax.map(one_image, jnp.arange(MICRO * IMGS, dtype=jnp.int32))
    early_states = jnp.stack([prior_base, prior_first]).reshape(2, MICRO, IMGS, 3, PX)
    final_states = jnp.stack([clean_last, prior_last]).reshape(2, MICRO, IMGS, 3, ROWS2, WIN2)
    return (early_states, final_states)
```

```python
import math

import jax
import jax.numpy as jnp
from jax import lax
from jax.sharding import PartitionSpec as P

HD = 64


def rms_scale(hidden, gain):
    return hidden * lax.rsqrt(jnp.mean(hidden * hidden, axis=-1, keepdims=True) + 1e-06) * gain


def alpha_bar(step):
    frac = (step.astype(jnp.float32) / 1000.0 + 0.008) / 1.008
    return jnp.cos(frac * (math.pi / 2)) ** 2


def time_embed(steps, w_time):
    half = w_time.shape[0] // 2
    freqs = jnp.exp(-math.log(10000.0) * jnp.arange(half, dtype=jnp.float32) / half)
    angle = steps.astype(jnp.float32)[:, None] * freqs[None]
    embed = jnp.concatenate([jnp.sin(angle), jnp.cos(angle)], axis=1).astype(jnp.bfloat16)
    return jnp.dot(embed, w_time, preferred_element_type=jnp.float32)


def section(planes, noisy, row_ok, keyval, valid, steps, weights):
    w_in, w_time, gains, w_conv, w_query, w_out, w_head = weights
    count, chans, high, wide = planes.shape
    width = w_query.shape[0]
    heads = width // HD
    pixels = planes.transpose(0, 2, 3, 1)
    hidden = jnp.einsum("bhwc,cd->bhwd", pixels, w_in, preferred_element_type=jnp.float32)
    hidden = hidden + time_embed(steps, w_time)[:, None, None, :]
    active = jax.nn.silu(rms_scale(hidden, gains[0]))
    active = jnp.where(row_ok[:, :, None, None], active, 0.0).astype(jnp.bfloat16)
    padded = jnp.pad(active, ((0, 0), (0, 0), (1, 1), (0, 0)))
    taps = [padded[:, tap // 3 : tap // 3 + high - 2, tap % 3 : tap % 3 + wide, :] for tap in range(9)]
    stacked = jnp.concatenate(taps, axis=-1)
    conv = jnp.einsum(
        "bhwk,kd->bhwd", stacked, w_conv.reshape(9 * width, width), preferred_element_type=jnp.float32
    )
    hidden = (hidden[:, 1:-1] + conv).reshape(count, -1, width)
    query = jnp.dot(
        rms_scale(hidden, gains[1]).astype(jnp.bfloat16), w_query, preferred_element_type=jnp.float32
    )
    query = (query * HD**-0.5).astype(jnp.bfloat16).reshape(count, -1, heads, HD)
    keys = keyval[:, :, :width].reshape(count, -1, heads, HD)
    values = keyval[:, :, width:].reshape(count, -1, heads, HD)
    scores = jnp.einsum("bphd,blhd->bhpl", query, keys, preferred_element_type=jnp.float32)
    scores = jnp.where(valid[:, None, None, :], scores, -1e30)
    mix = jax.nn.softmax(scores, axis=-1).astype(jnp.bfloat16)
    mixed = jnp.einsum("bhpl,blhd->bphd", mix, values, preferred_element_type=jnp.float32)
    mixed = mixed.reshape(count, -1, width).astype(jnp.bfloat16)
    hidden = hidden + jnp.dot(mixed, w_out, preferred_element_type=jnp.float32)
    normed = rms_scale(hidden, gains[2]).astype(jnp.bfloat16)
    eps = jnp.einsum("bpc,ce->bep", normed, w_head, preferred_element_type=jnp.float32)
    level = alpha_bar(steps)[:, None, None]
    earlier = alpha_bar(steps - 50)[:, None, None]
    noisy = noisy.reshape(count, 3, -1).astype(jnp.float32)
    clean = jnp.clip((noisy - jnp.sqrt(1.0 - level) * eps) / jnp.sqrt(level), -1.0, 1.0)
    prior = jnp.sqrt(earlier) * clean + jnp.sqrt(1.0 - earlier) * eps
    return clean.astype(jnp.bfloat16), prior.astype(jnp.bfloat16)


def shards(
    text_states,
    token_ids,
    step_ids,
    base_noise,
    upscale_noise,
    final_noise,
    t5_gain,
    base_keyval,
    upscale_keyval,
    base_input,
    base_time,
    base_gain,
    base_conv,
    base_query,
    base_output,
    base_head,
    upscale_input,
    upscale_time,
    upscale_gain,
    upscale_conv,
    upscale_query,
    upscale_output,
    upscale_head,
):
    groups = lax.axis_size("space")
    segments = lax.axis_size("segment")
    ratio = groups // segments
    segment = lax.axis_index("segment")
    place = lax.axis_index("space")
    micro, _, ltxt, dt5 = text_states.shape
    pixels = base_noise.shape[3]
    rows_dev, cols = final_noise.shape[3:]
    side = cols
    quarter = side // 4
    rows_total = rows_dev * groups
    tall = rows_total // side
    band = side // segments
    cond_dev = side // groups
    valid_all = token_ids != 0
    base_weights = (base_input, base_time, base_gain, base_conv, base_query, base_output, base_head)
    stacked = (
        upscale_input,
        upscale_time,
        upscale_gain,
        upscale_conv,
        upscale_query,
        upscale_output,
        upscale_head,
    )
    first_weights = tuple(weight[0] for weight in stacked)
    last_weights = tuple(weight[1] for weight in stacked)

    mine = lax.dynamic_slice_in_dim(final_noise, ratio * segment, ratio, 1)
    above = lax.ppermute(mine[:, :, :, -1], "space", [(i, i + 1) for i in range(groups - 1)])
    below = lax.ppermute(mine[:, :, :, 0], "space", [(i + 1, i) for i in range(groups - 1)])

    context = rms_scale(text_states.reshape(micro * ltxt, dt5).astype(jnp.float32), t5_gain)
    context = context.astype(jnp.bfloat16)

    def project(weight):
        out = jnp.dot(context, weight, preferred_element_type=jnp.float32).astype(jnp.bfloat16)
        return out.reshape(micro, ltxt, -1)

    key_last = project(upscale_keyval[1])
    pairs = [
        [
            (s * groups + ratio * q + r, q * groups + ratio * s + (r + k) % ratio)
            for s in range(segments)
            for q in range(segments)
            for r in range(ratio)
        ]
        for k in range(ratio)
    ]
    axes = ("segment", "space")
    keys_got = [lax.ppermute(key_last, axes, pairs[k]) for k in range(ratio)]
    key_base = project(base_keyval)
    key_first = project(upscale_keyval[0])
    own_valid = lax.dynamic_index_in_dim(valid_all, place, 1, keepdims=False)

    base_planes = base_noise.reshape(micro, 3, side, side)
    corner = jnp.pad(base_planes[:, :, : quarter + 1, : quarter + 1], ((0, 0), (0, 0), (1, 0), (0, 0)))
    corner_ok = jnp.broadcast_to((jnp.arange(quarter + 2) > 0)[None], (micro, quarter + 2))
    clean_corner, _ = section(
        corner, corner[:, :, 1:-1], corner_ok, key_base, own_valid, step_ids[0], base_weights
    )
    clean_corner = clean_corner.reshape(micro, 3, quarter, quarter + 1)[:, :, :, :quarter]

    rise = side // quarter
    cond_first = jnp.repeat(jnp.repeat(clean_corner, rise, axis=2), rise, axis=3)
    first_planes = jnp.concatenate([upscale_noise.reshape(micro, 3, side, side), cond_first], axis=1)
    first_planes = jnp.pad(first_planes, ((0, 0), (0, 0), (2, 2), (0, 0)))
    first_planes = lax.dynamic_slice_in_dim(first_planes, segment * band, band + 4, 2)
    row_at = segment * band - 2 + jnp.arange(band + 4)
    first_ok = jnp.broadcast_to(((row_at >= 0) & (row_at < side))[None], (micro, band + 4))
    clean_first, prior_first = section(
        first_planes,
        first_planes[:, :3, 1:-1],
        first_ok,
        key_first,
        own_valid,
        step_ids[1],
        first_weights,
    )
    clean_got = [lax.ppermute(clean_first, axes, pairs[k]) for k in range(ratio)]
    prior_first = prior_first.reshape(micro, 3, band + 2, side)[:, :, 1:-1].reshape(micro, 3, -1)

    main = jnp.pad(base_planes, ((0, 0), (0, 0), (1, 1), (0, 0)))
    main = lax.dynamic_slice_in_dim(main, segment * band, band + 2, 2)
    row_at = segment * band - 1 + jnp.arange(band + 2)
    main_ok = jnp.broadcast_to(((row_at >= 0) & (row_at < side))[None], (micro, band + 2))
    _, prior_base = section(
        main, main[:, :, 1:-1], main_ok, key_base, own_valid, step_ids[0], base_weights
    )
    early_states = jnp.stack([prior_base, prior_first])[:, :, None]

    phase = place % ratio
    ordered = [(phase - k) % ratio for k in range(ratio)]
    noise = jnp.concatenate([above[:, :, :, None], mine, below[:, :, :, None]], axis=3)
    row_at = place * rows_dev - 1 + jnp.arange(rows_dev + 2)
    last_ok = jnp.broadcast_to(((row_at >= 0) & (row_at < rows_total))[None], (micro, rows_dev + 2))
    final = jnp.zeros((2, micro, ratio, 3, rows_dev, cols), jnp.bfloat16)
    for k in range(ratio):
        r = ordered[k]
        clean_rows = clean_got[k].reshape(micro, 3, band + 2, side)
        clean_rows = lax.dynamic_slice_in_dim(clean_rows, phase * cond_dev, cond_dev + 2, 2)
        cond = jnp.repeat(clean_rows, tall, axis=2)[:, :, tall - 1 : tall + rows_dev + 1]
        own = lax.dynamic_index_in_dim(noise, r, 1, keepdims=False)
        valid = lax.dynamic_index_in_dim(valid_all, segment * ratio + r, 1, keepdims=False)
        clean, prior = section(
            jnp.concatenate([own, cond], axis=1),
            own[:, :, 1:-1],
            last_ok,
            keys_got[k],
            valid,
            step_ids[2],
            last_weights,
        )
        pair = jnp.stack([clean, prior]).reshape(2, micro, 1, 3, rows_dev, cols)
        final = lax.dynamic_update_slice_in_dim(final, pair, r, 2)
    return early_states, final


def solution(mesh):
    placed = (
        P(None, "space", None, None),
        P(),
        P(),
        P(None, "space", None, None),
        P(None, "space", None, None),
        P(None, None, None, "space", None),
    ) + (P(),) * 17
    return jax.shard_map(
        shards,
        mesh=mesh,
        in_specs=placed,
        out_specs=(
            P(None, None, "space", None, "segment"),
            P(None, None, "segment", None, "space", None),
        ),
        check_vma=False,
    )
```

```python
import functools
import math

import jax
import jax.numpy as jnp
from jax import lax
from jax.experimental import pallas as pl
from jax.experimental.pallas import tpu as pltpu
from jax.sharding import PartitionSpec as P

HD = 64
LTXT = 128
VMEM_ALL = 67043328
LOG2E = math.log2(math.e)


NT = (((1,), (1,)), ((), ()))


def unit(x):
    return x * lax.rsqrt(jnp.sum(x * x, axis=-1, keepdims=True) * (1.0 / x.shape[-1]) + 1e-06)


def silu(x):
    return x * (0.5 + 0.5 * jnp.tanh(0.5 * x))


def fdot(a, b):
    return jnp.dot(a, b, preferred_element_type=jnp.float32)


def plane_rows(ref, at, size):
    parts = [ref[c, :, pl.ds(at, size)].astype(jnp.float32) for c in range(ref.shape[0])]
    return jnp.concatenate(parts, axis=0)


def mix_rows(rows, m, micro, total):
    zero = jnp.zeros_like(rows[0])
    out = [row if n == m else zero for row in rows for n in range(micro)]
    if total > len(out):
        out.append(jnp.zeros((total - len(out), rows[0].shape[1]), rows[0].dtype))
    return jnp.concatenate(out, axis=0)


def spread_cols(act, side, pad, dst):
    count, chans = act.shape
    pad[8 : 8 + count] = act
    col = lax.rem(lax.broadcasted_iota(jnp.int32, (count, chans), 0), side)
    left = jnp.where(col == 0, 0.0, pad[7 : 7 + count])
    right = jnp.where(col == side - 1, 0.0, pad[9 : 9 + count])
    dst[:, :chans] = left.astype(jnp.bfloat16)
    dst[:, chans : 2 * chans] = act.astype(jnp.bfloat16)
    dst[:, 2 * chans :] = right.astype(jnp.bfloat16)


def pair_keys(keys, vals):
    first = lax.broadcasted_iota(jnp.int32, keys.shape, 1) < HD
    keys, vals = keys.astype(jnp.float32), vals.astype(jnp.float32)
    kmask = jnp.concatenate([jnp.where(first, keys, 0.0), jnp.where(first, 0.0, keys)], axis=0)
    upper = jnp.concatenate([jnp.where(first, vals, 0.0), jnp.where(first, 1.0, 0.0)], axis=1)
    lower = jnp.concatenate([jnp.where(first, 0.0, vals), jnp.where(first, 0.0, 1.0)], axis=1)
    return kmask.astype(jnp.bfloat16), jnp.concatenate([upper, lower], axis=0).astype(jnp.bfloat16)


def attend_pair(query, kmask, vaug, bias):
    lanes = query.shape[1]
    half = kmask.shape[0] // 2
    scores = lax.dot_general(query, kmask, NT, preferred_element_type=jnp.float32) + bias
    probs = []
    for e in range(2):
        part = scores[:, e * half : (e + 1) * half]
        probs.append(jnp.exp2(part - jnp.max(part, axis=-1, keepdims=True)).astype(jnp.bfloat16))
    both = fdot(jnp.concatenate(probs, axis=1), vaug)
    return (both[:, :lanes] / both[:, lanes:]).astype(jnp.bfloat16)


def key_bias(ids_ref, m, who):
    bias = jnp.where(ids_ref[m, pl.ds(who, 1)] == 0, -1e30, 0.0)
    return jnp.concatenate([bias, bias], axis=1)


def back_part(h1, micro, keyvals, biases, gain1, gain2, w_query, w_out, head_rows):
    count, width = h1.shape
    each = count // micro
    query = fdot((unit(h1) * gain1).astype(jnp.bfloat16), w_query)
    query = (query * (HD**-0.5 * LOG2E)).astype(jnp.bfloat16)
    mixed = []
    for m in range(micro):
        cols = []
        for g in range(width // (2 * HD)):
            at = slice(2 * HD * g, 2 * HD * (g + 1))
            kmask, vaug = pair_keys(keyvals[m](at), keyvals[m](slice(width + at.start, width + at.stop)))
            cols.append(attend_pair(query[m * each : (m + 1) * each, at], kmask, vaug, biases[m]))
        mixed.append(jnp.concatenate(cols, axis=1) if len(cols) > 1 else cols[0])
    h2 = h1 + fdot(jnp.concatenate(mixed, axis=0), w_out)
    normed = (unit(h2) * gain2).astype(jnp.bfloat16)
    eps = 0.0
    for m in range(micro):
        rows = mix_rows(head_rows, m, micro, 16).astype(jnp.bfloat16)
        eps = eps + lax.dot_general(
            rows, normed[m * each : (m + 1) * each], NT, preferred_element_type=jnp.float32
        )
    return eps[: 3 * micro]


def alpha_bar(step):
    frac = (step / 1000.0 + 0.008) / 1.008
    return jnp.cos(frac * (math.pi / 2)) ** 2


def embed(step_ref, sec, chans):
    lane = lax.broadcasted_iota(jnp.int32, (16, chans), 1)
    row = lax.broadcasted_iota(jnp.int32, (16, chans), 0)
    half = chans // 2
    steps = jnp.zeros((16, chans), jnp.float32)
    for m in range(step_ref.shape[0]):
        steps = jnp.where(row == m, step_ref[m, sec].astype(jnp.float32), steps)
    angle = steps * jnp.exp(lax.rem(lane, half).astype(jnp.float32) * (-math.log(10000.0) / half))
    return jnp.where(lane < half, jnp.sin(angle), jnp.cos(angle)).astype(jnp.bfloat16)


def levels(step_ref, m, sec):
    step = jnp.full((8, 128), step_ref[m, sec].astype(jnp.float32))
    level, earlier = alpha_bar(step), alpha_bar(step - 50.0)
    out = (jnp.sqrt(1.0 - level), 1.0 / jnp.sqrt(level), jnp.sqrt(earlier), jnp.sqrt(1.0 - earlier))
    return [part[:1, :1] for part in out]


def denoise(noise, eps, step_ref, sec):
    micro = step_ref.shape[0]
    which = lax.rem(lax.broadcasted_iota(jnp.int32, eps.shape, 0), micro)
    table = [levels(step_ref, m, sec) for m in range(micro)]

    def scalar(n):
        out = jnp.broadcast_to(table[0][n], eps.shape)
        for m in range(1, micro):
            out = jnp.where(which == m, table[m][n], out)
        return out

    clean = jnp.clip((noise - scalar(0) * eps) * scalar(1), -1.0, 1.0)
    return clean, scalar(2) * clean + scalar(3) * eps


def begin(pairs, sems):
    copies = [pltpu.make_async_copy(src, dst, sems.at[n]) for n, (src, dst) in enumerate(pairs)]
    for copy in copies:
        copy.start()
    return copies


def front_kernel(step_ref, *refs):
    (
        text_hbm,
        t5_hbm,
        ids_hbm,
        base_x_hbm,
        first_x_hbm,
        base_in_hbm,
        base_gain_hbm,
        base_head_hbm,
        up_in_hbm,
        up_gain_hbm,
        up_head_hbm,
        up_time_hbm,
        up_conv_hbm,
        up_query_hbm,
        up_out_hbm,
        time_hbm,
        conv_hbm,
        query_hbm,
        out_hbm,
        kv_base_hbm,
        kv_up_hbm,
    ) = refs[:21]
    kv_base_out, load_out, next_out = refs[21:24]
    (
        text,
        t5_ref,
        ids_ref,
        base_x_ref,
        first_x_ref,
        base_in_ref,
        base_gain_ref,
        base_head_ref,
        up_in_ref,
        up_gain_ref,
        up_head_ref,
        up_time_ref,
        up_conv_ref,
        up_query_ref,
        up_out_ref,
        w_time,
        conv,
        w_query,
        w_out,
        kv_w,
        context,
        kv_first,
        pad_base,
        taps,
        wide_x,
        pad_first,
        cols_first,
        sems,
    ) = refs[24:]
    seg, place = lax.axis_index("segment"), lax.axis_index("space")
    segments = lax.axis_size("segment")
    rows_text, dt5 = text.shape
    micro = base_x_ref.shape[1]
    ltxt = rows_text // micro
    cb, cs = base_gain_ref.shape[1], up_gain_ref.shape[2]
    px = base_x_ref.shape[2]
    side = math.isqrt(px)
    quarter = side // 4
    band = side // segments
    bf, f32 = jnp.bfloat16, jnp.float32
    step = kv_w.shape[2]
    n_base = kv_base_hbm.shape[1] // step
    chunks = [(kv_base_hbm.at[:, n * step : (n + 1) * step], kv_w.at[n]) for n in range(n_base)]
    chunks += [(kv_up_hbm.at[n], kv_w.at[n_base + n]) for n in range(2)]
    small = (
        (ids_hbm, ids_ref),
        (base_x_hbm, base_x_ref),
        (first_x_hbm, first_x_ref),
        (base_in_hbm, base_in_ref),
        (base_gain_hbm, base_gain_ref),
        (base_head_hbm, base_head_ref),
        (up_in_hbm, up_in_ref),
        (up_gain_hbm, up_gain_ref),
        (up_head_hbm, up_head_ref),
        (up_time_hbm.at[0], up_time_ref),
        (up_conv_hbm.at[0], up_conv_ref),
        (up_query_hbm.at[0], up_query_ref),
        (up_out_hbm.at[0], up_out_ref),
        (time_hbm, w_time),
    )
    late = ((conv_hbm, conv), (query_hbm, w_query), (out_hbm, w_out))
    copies = begin([(t5_hbm, t5_ref), (text_hbm, text)] + chunks + list(small) + list(late), sems)
    after = 2 + len(chunks)

    copies[0].wait()
    copies[1].wait()
    gain = t5_ref[...]

    def prepare(i, carry):
        at = pl.multiple_of(i * 16, 16)
        x = text[pl.ds(at, 16)].astype(f32)
        context[pl.ds(at, 16)] = (unit(x) * gain).astype(bf)
        return carry

    lax.fori_loop(0, rows_text // 16, prepare, 0)
    for n in range(n_base + 2):
        copies[2 + n].wait()
        half = dt5 // 2
        out = fdot(context[:, :half], kv_w[n, :half]) + fdot(context[:, half:], kv_w[n, half:])
        out = out.astype(bf)
        if n < n_base:
            kv_base_out[:, n * step : (n + 1) * step] = out
        elif n == n_base:
            kv_first[...] = out
        else:
            load_out[: micro * ltxt] = out

    for copy in copies[after : after + len(small)]:
        copy.wait()
    biases = [key_bias(ids_ref, m, place) for m in range(micro)]

    tall = quarter + 1
    temb = fdot(embed(step_ref, 0, cb), w_time[...])
    base_rows = [base_in_ref[c : c + 1].astype(f32) for c in range(3)]
    lanes = 128 * ((tall * side + 127) // 128)
    x_t = jnp.concatenate([plane_rows(base_x_ref, 0, lanes), jnp.zeros((2, lanes), f32)], axis=0)
    x_t = jnp.transpose(x_t)[: tall * side].astype(bf)
    pad_base[: 8 + side] = jnp.zeros((8 + side, cb), f32)
    edge = lax.broadcasted_iota(jnp.int32, (quarter, cb), 0) == 0
    corner_h = []
    for m in range(micro):
        h0 = fdot(x_t, mix_rows(base_rows, m, micro, 8).astype(bf)) + temb[m : m + 1]
        pad_base[8 + side : 8 + side + tall * side] = silu(unit(h0) * base_gain_ref[0:1])
        corner_h.append(
            jnp.concatenate([h0[side * h : side * h + quarter] for h in range(quarter)], axis=0)
        )
        for r in range(quarter + 1):
            for b in range(3):
                lo = pad_base[8 + side * r + b - 1 : 8 + side * r + b - 1 + quarter]
                hi = pad_base[8 + side * (r + 1) + b - 1 : 8 + side * (r + 1) + b - 1 + quarter]
                if b == 0:
                    lo, hi = jnp.where(edge, 0.0, lo), jnp.where(edge, 0.0, hi)
                both = jnp.concatenate([lo, hi], axis=0).astype(bf)
                for a in range(3):
                    h = r - a
                    if h % 2 == 0 and 0 <= h < quarter:
                        at = m * quarter * quarter + h * quarter
                        taps[at : at + 2 * quarter, (3 * a + b) * cb : (3 * a + b + 1) * cb] = both
    copies[after + len(small)].wait()
    h1 = jnp.concatenate(corner_h, axis=0) + fdot(taps[...], conv[...])
    copies[after + len(small) + 1].wait()
    copies[after + len(small) + 2].wait()
    keyvals = [lambda at, m=m: kv_base_out[m * ltxt : (m + 1) * ltxt, at] for m in range(micro)]
    head_rows = [base_head_ref[c : c + 1].astype(f32) for c in range(3)]
    eps = back_part(
        h1, micro, keyvals, biases, base_gain_ref[1:2], base_gain_ref[2:3], w_query[...], w_out[...], head_rows
    )
    noise = plane_rows(base_x_ref, 0, lanes)
    noise = jnp.concatenate([noise[:, side * h : side * h + quarter] for h in range(quarter)], axis=1)
    corner, _ = denoise(noise, eps, step_ref, 0)

    near = 128 * ((2 * side + 127) // 128)
    window = near + band * side + near
    wide_x[...] = jnp.zeros_like(wide_x)
    wide_x[: 3 * micro, near : near + px] = plane_rows(first_x_ref, 0, px)
    x_win = wide_x[:, pl.ds(pl.multiple_of(seg * (band * side), 128), window)]
    spot = lax.broadcasted_iota(jnp.int32, (quarter * quarter, window), 0)
    pixel = lax.broadcasted_iota(jnp.int32, (quarter * quarter, window), 1) + (seg * band * side - near)
    rise = side // quarter
    hit = (lax.shift_right_arithmetic(pixel, (side * rise).bit_length() - 1) == lax.div(spot, quarter)) & (
        lax.div(lax.rem(pixel + 4 * px, side), rise) == lax.rem(spot, quarter)
    )
    corner16 = jnp.concatenate([corner, jnp.zeros((16 - 3 * micro, corner.shape[1]), f32)], axis=0).astype(bf)
    cond = fdot(corner16, jnp.where(hit, 1.0, 0.0).astype(bf))[:8]
    x_t = jnp.transpose(jnp.concatenate([x_win, cond], axis=0))
    skip = near - 2 * side
    total = (band + 4) * side
    x_t = x_t[skip : skip + total].astype(bf)
    temb = fdot(embed(step_ref, 1, cs), up_time_ref[...])
    up_rows = [up_in_ref[c, 0:1].astype(f32) for c in range(6)]
    row = lax.div(lax.broadcasted_iota(jnp.int32, (total, cs), 0), side) + (seg * band - 2)
    inside = (row >= 0) & (row < side)
    kept = (band + 2) * side
    first_h, lhs = [], []
    for m in range(micro):
        rhs = jnp.concatenate(
            [mix_rows(up_rows[:3], m, micro, 8), mix_rows(up_rows[3:], m, micro, 8)], axis=0
        ).astype(bf)
        h0 = fdot(x_t, rhs) + temb[m : m + 1]
        act = jnp.where(inside, silu(unit(h0) * up_gain_ref[0, 0:1]), 0.0)
        spread_cols(act, side, pad_first, cols_first.at[m])
        first_h.append(h0[side : side + kept])
        lhs.append(
            jnp.concatenate([cols_first[m, a * side : a * side + kept] for a in range(3)], axis=1)
        )
    h1 = jnp.concatenate(first_h, axis=0) + fdot(jnp.concatenate(lhs, axis=0), up_conv_ref[...].reshape(9 * cs, cs))
    keyvals = [lambda at, m=m: kv_first[m * ltxt : (m + 1) * ltxt, at] for m in range(micro)]
    head_rows = [up_head_ref[c, 0:1].astype(f32) for c in range(3)]
    eps = back_part(
        h1, micro, keyvals, biases, up_gain_ref[1, 0:1], up_gain_ref[2, 0:1], up_query_ref[...], up_out_ref[...],
        head_rows,
    )
    noise = x_win[: 3 * micro, near - side : near - side + kept]
    clean, prior = denoise(noise, eps, step_ref, 1)
    for c in range(3):
        next_out[c] = prior[c * micro : (c + 1) * micro, side : side + band * side].astype(bf)
    wide = load_out.shape[1]
    blocks = (load_out.shape[0] - micro * ltxt) // 16
    clean = jnp.concatenate([clean, jnp.zeros((3 * micro, blocks * wide - kept), f32)], axis=1)
    clean = jnp.concatenate([clean, jnp.zeros((16 - 3 * micro, blocks * wide), f32)], axis=0).astype(bf)
    for b in range(blocks):
        at = micro * ltxt + 16 * b
        load_out[at : at + 16] = clean[:, b * wide : (b + 1) * wide]


def base_kernel(step_ref, *refs):
    hbm, early_ref, vmem, extra = refs[:11], refs[11], refs[12:23], refs[23:]
    x_ref, w_in_ref, gain_ref, head_ref, time_ref, ids_ref, next_ref, kv_ref, conv, w_query, w_out = vmem
    wide_x, pad, cols, sems = extra
    seg, place = lax.axis_index("segment"), lax.axis_index("space")
    segments = lax.axis_size("segment")
    micro, px = x_ref.shape[1:]
    side = math.isqrt(px)
    band = side // segments
    ltxt = kv_ref.shape[0] // micro
    bf, f32 = jnp.bfloat16, jnp.float32
    copies = begin(list(zip(hbm, vmem)), sems)
    for copy in copies[:5]:
        copy.wait()
    chans = gain_ref.shape[1]
    near = 128 * ((side + 127) // 128)
    window = near + band * side + near
    wide_x[...] = jnp.zeros_like(wide_x)
    wide_x[: 3 * micro, near : near + px] = plane_rows(x_ref, 0, px)
    x_win = wide_x[:, pl.ds(pl.multiple_of(seg * (band * side), 128), window)]
    total = (band + 2) * side
    x_t = jnp.transpose(x_win)[near - side : near - side + total].astype(bf)
    temb = fdot(embed(step_ref, 0, chans), time_ref[...])
    rows = [w_in_ref[c : c + 1].astype(f32) for c in range(3)]
    row = lax.div(lax.broadcasted_iota(jnp.int32, (total, chans), 0), side) + (seg * band - 1)
    inside = (row >= 0) & (row < side)
    kept = band * side
    hid, lhs = [], []
    for m in range(micro):
        h0 = fdot(x_t, mix_rows(rows, m, micro, 8).astype(bf)) + temb[m : m + 1]
        act = jnp.where(inside, silu(unit(h0) * gain_ref[0:1]), 0.0)
        spread_cols(act, side, pad, cols.at[m])
        hid.append(h0[side : side + kept])
        lhs.append(jnp.concatenate([cols[m, a * side : a * side + kept] for a in range(3)], axis=1))
    for copy in copies[5:9]:
        copy.wait()
    h1 = jnp.concatenate(hid, axis=0) + fdot(jnp.concatenate(lhs, axis=0), conv[...])
    copies[9].wait()
    copies[10].wait()
    biases = [key_bias(ids_ref, m, place) for m in range(micro)]
    keyvals = [lambda at, m=m: kv_ref[m * ltxt : (m + 1) * ltxt, at] for m in range(micro)]
    head_rows = [head_ref[c : c + 1].astype(f32) for c in range(3)]
    eps = back_part(
        h1, micro, keyvals, biases, gain_ref[1:2], gain_ref[2:3], w_query[...], w_out[...], head_rows
    )
    _, prior = denoise(x_win[: 3 * micro, near : near + kept], eps, step_ref, 0)
    for c in range(3):
        early_ref[0, c] = prior[c * micro : (c + 1) * micro].astype(bf)
    early_ref[1] = next_ref[...]


def like(array, index=None):
    shape = array.shape if index is None else array.shape[1:]
    return pltpu.VMEM(shape, array.dtype)


def front_call(segments, steps, ids, base_x, first_x, t5, base_w, up_w, text, kv_base_w, kv_up_w):
    base_in, base_time, base_gain, base_conv, base_query, base_output, base_head = base_w
    up_in, up_time, up_gain, up_conv, up_query, up_out, up_head = up_w
    rows_text, dt5 = text.shape
    micro, px = base_x.shape[1:]
    side = math.isqrt(px)
    band = side // segments
    quarter = side // 4
    cb, cs = base_gain.shape[1], up_gain.shape[2]
    step = kv_up_w.shape[2]
    chunks = kv_base_w.shape[1] // step + 2
    near = 128 * ((2 * side + 127) // 128)
    blocks = -(-((band + 2) * side) // step)
    bf, f32 = jnp.bfloat16, jnp.float32
    smem = pl.BlockSpec(memory_space=pltpu.SMEM)
    vmem = pl.BlockSpec(memory_space=pltpu.VMEM)
    hbm = pl.BlockSpec(memory_space=pltpu.HBM)
    whole = (text, t5, ids, base_x, first_x, base_in, base_gain, base_head, up_in, up_gain, up_head)
    cut = (up_time, up_conv, up_query, up_out)
    big = (base_time, base_conv, base_query, base_output)
    args = whole + cut + big + (kv_base_w, kv_up_w)
    return pl.pallas_call(
        front_kernel,
        out_shape=(
            jax.ShapeDtypeStruct((rows_text, 2 * cb), bf),
            jax.ShapeDtypeStruct((rows_text + 16 * blocks, step), bf),
            jax.ShapeDtypeStruct((3, micro, band * side), bf),
        ),
        in_specs=[smem] + [hbm] * len(args),
        out_specs=(vmem, vmem, vmem),
        scratch_shapes=[like(a) for a in whole]
        + [like(a, 0) for a in cut]
        + [like(a) for a in big]
        + [
            pltpu.VMEM((chunks, dt5, step), bf),
            pltpu.VMEM((rows_text, dt5), bf),
            pltpu.VMEM((rows_text, step), bf),
            pltpu.VMEM((16 + side + (quarter + 1) * side, cb), f32),
            pltpu.VMEM((micro * quarter * quarter, 9 * cb), bf),
            pltpu.VMEM((8, near + px + near), f32),
            pltpu.VMEM(((band + 4) * side + 16, cs), f32),
            pltpu.VMEM((micro, (band + 4) * side, 3 * cs), bf),
            pltpu.SemaphoreType.DMA((chunks + 19,)),
        ],
        compiler_params=pltpu.CompilerParams(vmem_limit_bytes=VMEM_ALL),
        cost_estimate=pl.CostEstimate(flops=5 * 10**9, bytes_accessed=22 * 10**6, transcendentals=10**6),
        name="text_and_first",
    )(steps, *args)


def base_call(segments, steps, ids, base_x, base_w, first_next, kv_base):
    base_in, base_time, base_gain, base_conv, base_query, base_output, base_head = base_w
    micro, px = base_x.shape[1:]
    side = math.isqrt(px)
    band = side // segments
    cb = base_gain.shape[1]
    near = 128 * ((side + 127) // 128)
    bf, f32 = jnp.bfloat16, jnp.float32
    smem = pl.BlockSpec(memory_space=pltpu.SMEM)
    vmem = pl.BlockSpec(memory_space=pltpu.VMEM)
    hbm = pl.BlockSpec(memory_space=pltpu.HBM)
    args = (base_x, base_in, base_gain, base_head, base_time, ids, first_next, kv_base, base_conv, base_query)
    args += (base_output,)
    return pl.pallas_call(
        base_kernel,
        out_shape=jax.ShapeDtypeStruct((2, 3, micro, band * side), bf),
        in_specs=[smem] + [hbm] * len(args),
        out_specs=vmem,
        scratch_shapes=[like(a) for a in args]
        + [
            pltpu.VMEM((8, near + px + near), f32),
            pltpu.VMEM(((band + 2) * side + 16, cb), f32),
            pltpu.VMEM((micro, (band + 2) * side, 3 * cb), bf),
            pltpu.SemaphoreType.DMA((len(args),)),
        ],
        compiler_params=pltpu.CompilerParams(vmem_limit_bytes=VMEM_ALL),
        cost_estimate=pl.CostEstimate(flops=4 * 10**9, bytes_accessed=7 * 10**6, transcendentals=10**6),
        name="base_section",
    )(steps, *args)


def last_kernel(ratio, tall, step_ref, *refs):
    hbm, out_ref = refs[: 11 + ratio], refs[11 + ratio]
    ids_ref, mine_ref, near_ref, far_ref, w_in_ref, gain_ref, head_ref, w_time_ref, conv_ref, query_ref, out_w_ref = refs[
        12 + ratio : 23 + ratio
    ]
    load, inbig, headbig, wpair, wq2, wo2, cond_pick, act, even, odd, hid, turn, sems = refs[23 + ratio :]
    seg, place = lax.axis_index("segment"), lax.axis_index("space")
    groups = lax.axis_size("space")
    micro = step_ref.shape[0]
    span = load.shape[1] - micro * LTXT
    own = pl.ds(seg * ratio, ratio)
    pairs_io = [(hbm[4], w_in_ref), (hbm[5], gain_ref), (hbm[6], head_ref)]
    pairs_io += [(hbm[7 + n].at[1], ref) for n, ref in enumerate((w_time_ref, conv_ref, query_ref, out_w_ref))]
    pairs_io += [(hbm[0], ids_ref)]
    pairs_io += [(hbm[1 + n].at[:, own], ref) for n, ref in enumerate((mine_ref, near_ref, far_ref))]
    pairs_io += [(hbm[11 + k], load.at[k]) for k in range(ratio)]
    copies = begin(pairs_io, sems)
    chans = query_ref.shape[0]
    wide, high = mine_ref.shape[3:]
    ltxt = LTXT
    planes = 3 * wide
    phase = lax.rem(place, ratio)
    odd_place = lax.rem(place, 2) == 1
    cond_dev = high // tall
    pairs = wide // 2
    rows = high + 16
    lane2 = 2 * chans

    for copy in copies[:7]:
        copy.wait()
    row_id = lax.broadcasted_iota(jnp.int32, (2 * planes, chans), 0)
    stack = jnp.concatenate(
        [jnp.broadcast_to(w_in_ref[c, 1:2].astype(jnp.float32), (wide, chans)) for c in range(6)], axis=0
    )
    heads3 = jnp.concatenate(
        [jnp.broadcast_to(head_ref[c, 1:2].astype(jnp.float32), (wide, chans)) for c in range(3)], axis=0
    )
    for w in range(wide):
        here = lax.rem(row_id, wide) == w
        inbig[:, w * chans : (w + 1) * chans] = jnp.where(here, stack, 0.0).astype(jnp.bfloat16)
        headbig[:, w * chans : (w + 1) * chans] = jnp.where(here[:planes], heads3, 0.0).astype(jnp.bfloat16)
    zero_tap = jnp.zeros((chans, chans), jnp.bfloat16)
    for d in range(4):
        for a in range(3):
            at = (d * 3 + a) * chans
            wpair[at : at + chans, :chans] = conv_ref[3 * a + d] if d < 3 else zero_tap
            wpair[at : at + chans, chans:] = conv_ref[3 * a + d - 1] if d > 0 else zero_tap
    for dst, src in ((wq2, query_ref), (wo2, out_w_ref)):
        dst[:chans, :chans] = src[...]
        dst[:chans, chans:] = zero_tap
        dst[chans:, :chans] = zero_tap
        dst[chans:, chans:] = src[...]
    strip = cond_pick.shape[0] // 3
    pick_row = lax.broadcasted_iota(jnp.int32, (strip, planes), 0)
    pick_lane = lax.broadcasted_iota(jnp.int32, (strip, planes), 1)
    for c in range(3):
        hit = (pick_lane == c * wide + lax.rem(pick_row, wide))
        cond_pick[c * strip : (c + 1) * strip] = jnp.where(hit, 1.0, 0.0).astype(jnp.bfloat16)
    turn[...] = jnp.zeros_like(turn)
    even[0] = jnp.zeros_like(even[0])
    odd[pairs] = jnp.zeros_like(odd[pairs])

    temb = fdot(embed(step_ref, 2, chans), w_time_ref[...])
    top_ok = jnp.where(place > 0, 1.0, 0.0)
    low_ok = jnp.where(place < groups - 1, 1.0, 0.0)
    gain0, gain1, gain2 = gain_ref[0, 1:2], gain_ref[1, 1:2], gain_ref[2, 1:2]
    key_lane = lax.broadcasted_iota(jnp.int32, (ltxt, chans), 1)
    first_head = key_lane < HD
    inv = 1.0 / chans

    tile = lambda n: lax.div(lax.broadcasted_iota(jnp.int32, (lane2, lane2), n), chans)
    ones2 = jnp.where(tile(0) == tile(1), 1.0, 0.0).astype(jnp.bfloat16)
    gain0, gain1, gain2 = (jnp.concatenate([g, g], axis=1) for g in (gain0, gain1, gain2))

    def norm(x):
        total = fdot((x * x).astype(jnp.bfloat16), ones2)
        return x * lax.rsqrt(total * inv + 1e-06)

    tables = [levels(step_ref, m, 2) for m in range(micro)]
    for copy in copies[7:]:
        copy.wait()

    def image(i, carry):
        m = lax.div(i, ratio)
        k = lax.rem(i, ratio)
        r = lax.rem(phase - k + ratio, ratio)
        temb_m = jnp.where(m == 0, temb[0:1], temb[1:2])
        temb2 = jnp.concatenate([temb_m, temb_m], axis=1)

        turn[:planes, :high] = mine_ref[m, r].reshape(planes, high).astype(jnp.float32)
        body = jnp.transpose(turn[...])[:high, :planes]
        turn[:planes, :high] = near_ref[m, r].reshape(planes, high).astype(jnp.float32)
        near = jnp.transpose(turn[...])
        turn[:planes, :high] = far_ref[m, r].reshape(planes, high).astype(jnp.float32)
        far = jnp.transpose(turn[...])
        top = jnp.where(odd_place, near[high - 1 : high, :planes], far[high - 1 : high, :planes])
        low = jnp.where(odd_place, far[0:1, :planes], near[0:1, :planes])
        noise_rows = jnp.concatenate([body, top, low, jnp.zeros((14, planes), jnp.float32)], axis=0)

        blocks = [load[k, 2 * ltxt + 16 * b : 2 * ltxt + 16 * b + 8].astype(jnp.float32) for b in range(span // 16)]
        band_planes = jnp.concatenate(blocks, axis=1)[:, :strip]
        row_h = lax.broadcasted_iota(jnp.int32, (rows, strip), 0)
        lane_px = lax.broadcasted_iota(jnp.int32, (rows, strip), 1)
        need = jnp.where(
            row_h < high, 1 + lax.div(row_h, tall), jnp.where(row_h == high, 0, cond_dev + 1)
        ) + phase * cond_dev
        hit = lax.div(lane_px, wide) == need
        spread = []
        for c in range(3):
            plane = jnp.where(m == 0, band_planes[2 * c : 2 * c + 1], band_planes[2 * c + 1 : 2 * c + 2])
            spread.append(jnp.where(hit, jnp.broadcast_to(plane, (rows, strip)), 0.0).astype(jnp.bfloat16))
        cond_rows = jnp.dot(
            jnp.concatenate(spread, axis=1), cond_pick[...], preferred_element_type=jnp.float32
        )
        pixels = jnp.concatenate([noise_rows, cond_rows], axis=1).astype(jnp.bfloat16)

        def front(g, c2):
            for u in range(4):
                t = g * 4 + u
                h0 = fdot(pixels, inbig[:, pl.ds(pl.multiple_of(t * lane2, lane2), lane2)]) + temb2
                hid[t] = h0[:high]
                x = silu(norm(h0) * gain0)
                for par in range(2):
                    slot = u * 2 + par
                    at = slice(par * chans, (par + 1) * chans)
                    act[slot, 8 : 8 + high] = x[:high, at]
                    act[slot, 7:8] = x[high : high + 1, at] * top_ok
                    act[slot, 8 + high : 9 + high] = x[high + 1 : high + 2, at] * low_ok
                    wide3 = jnp.concatenate(
                        [act[slot, 7 + a : 7 + a + high].astype(jnp.bfloat16) for a in range(3)], axis=1
                    )
                    if par == 0:
                        odd[t] = wide3
                    else:
                        even[t + 1] = wide3
            return c2

        lax.fori_loop(0, pairs // 4, front, 0)

        keys = load[k, pl.ds(pl.multiple_of(m * ltxt, ltxt), ltxt), :chans].astype(jnp.float32)
        vals = load[k, pl.ds(pl.multiple_of(m * ltxt, ltxt), ltxt), chans:].astype(jnp.float32)
        ones = jnp.ones_like(keys)
        kmask = jnp.concatenate(
            [jnp.where(first_head, keys, 0.0), jnp.where(first_head, 0.0, keys)], axis=0
        ).astype(jnp.bfloat16)
        vaug = jnp.concatenate(
            [
                jnp.concatenate([jnp.where(first_head, vals, 0.0), jnp.where(first_head, ones, 0.0)], axis=1),
                jnp.concatenate([jnp.where(first_head, 0.0, vals), jnp.where(first_head, 0.0, ones)], axis=1),
            ],
            axis=0,
        ).astype(jnp.bfloat16)
        ids = ids_ref[m, pl.ds(seg * ratio + r, 1)]
        bias = jnp.where(ids == 0, -1e30, 0.0)
        bias = jnp.concatenate([bias, bias], axis=1)

        subs = 2
        each = 8
        m_rows = each * high

        def rest_of(g, c2):
            ats = [pl.multiple_of((g * subs + n) * each, each) for n in range(subs)]
            h1, q, sc, pr, mx, h2, n2 = [], [], [], [], [], [], []
            for at in ats:
                parts = [even[pl.ds(at, each)], odd[pl.ds(at, each)], even[pl.ds(at + 1, each)], odd[pl.ds(at + 1, each)]]
                lhs = jnp.concatenate([part.reshape(m_rows, 3 * chans) for part in parts], axis=1)
                h1.append(fdot(lhs, wpair[...]) + hid[pl.ds(at, each)].reshape(m_rows, lane2))
            for n in range(subs):
                qn = fdot((norm(h1[n]) * gain1).astype(jnp.bfloat16), wq2[...])
                q.append((qn * (HD**-0.5 * LOG2E)).astype(jnp.bfloat16))
            for n in range(subs):
                mixed = []
                for p in range(2):
                    scores = lax.dot_general(
                        q[n][:, p * chans : (p + 1) * chans], kmask, NT, preferred_element_type=jnp.float32
                    ) + bias
                    probs = []
                    for e in range(2):
                        s_e = scores[:, e * ltxt : (e + 1) * ltxt]
                        probs.append(jnp.exp2(s_e - jnp.max(s_e, axis=-1, keepdims=True)).astype(jnp.bfloat16))
                    both = fdot(jnp.concatenate(probs, axis=1), vaug)
                    mixed.append((both[:, :chans] / both[:, chans:]).astype(jnp.bfloat16))
                mx.append(jnp.concatenate(mixed, axis=1))
            for n in range(subs):
                h2.append(h1[n] + fdot(mx[n], wo2[...]))
            part = c2
            for n in range(subs):
                n2 = (norm(h2[n]) * gain2).astype(jnp.bfloat16).reshape(each, high, lane2)
                n2 = jnp.concatenate([n2[u] for u in range(each)], axis=1)
                at = pl.multiple_of(ats[n] * lane2, each * lane2)
                part = part + lax.dot_general(
                    headbig[:, pl.ds(at, each * lane2)], n2, NT, preferred_element_type=jnp.float32
                )
            return part

        eps = lax.fori_loop(0, pairs // (subs * each), rest_of, jnp.zeros((planes, high), jnp.float32))
        noise = mine_ref[m, r].reshape(planes, high).astype(jnp.float32)
        ca, cb, cc, cd = (jnp.where(m == 0, tables[0][n], tables[1][n]) for n in range(4))
        clean = jnp.clip((noise - ca * eps) * cb, -1.0, 1.0)
        prior = cc * clean + cd * eps
        out_ref[0, m, r] = clean.astype(jnp.bfloat16).reshape(3, wide, high)
        out_ref[1, m, r] = prior.astype(jnp.bfloat16).reshape(3, wide, high)
        return carry

    lax.fori_loop(0, micro * ratio, image, 0)


def last_call(ratio, tall, steps, ids, noise, near, far, loads, weights):
    w_in, w_time, gains, w_conv, w_query, w_out, head = weights
    micro, _, _, wide, high = noise.shape
    chans = w_query.shape[1]
    planes = 3 * wide
    pairs = wide // 2
    strip = 512
    smem = pl.BlockSpec(memory_space=pltpu.SMEM)
    vmem = pl.BlockSpec(memory_space=pltpu.VMEM)
    hbm = pl.BlockSpec(memory_space=pltpu.HBM)
    bf, f32 = jnp.bfloat16, jnp.float32
    args = (ids, noise, near, far, w_in, gains, head, w_time, w_conv, w_query, w_out) + tuple(loads)
    part = pltpu.VMEM((micro, ratio, 3, wide, high), bf)
    return pl.pallas_call(
        functools.partial(last_kernel, ratio, tall),
        out_shape=jax.ShapeDtypeStruct((2, micro, ratio, 3, wide, high), bf),
        in_specs=[smem] + [hbm] * len(args),
        out_specs=vmem,
        scratch_shapes=[like(ids), part, part, part, like(w_in), like(gains), like(head)]
        + [like(a, 0) for a in (w_time, w_conv, w_query, w_out)]
        + [
            pltpu.VMEM((ratio,) + loads[0].shape, bf),
            pltpu.VMEM((2 * planes, wide * chans), bf),
            pltpu.VMEM((planes, wide * chans), bf),
            pltpu.VMEM((12 * chans, 2 * chans), bf),
            pltpu.VMEM((2 * chans, 2 * chans), bf),
            pltpu.VMEM((2 * chans, 2 * chans), bf),
            pltpu.VMEM((3 * strip, planes), bf),
            pltpu.VMEM((8, high + 16, chans), f32),
            pltpu.VMEM((pairs + 1, high, 3 * chans), bf),
            pltpu.VMEM((pairs + 1, high, 3 * chans), bf),
            pltpu.VMEM((pairs, high, 2 * chans), f32),
            pltpu.VMEM((128, 128), f32),
            pltpu.SemaphoreType.DMA((len(args),)),
        ],
        compiler_params=pltpu.CompilerParams(vmem_limit_bytes=VMEM_ALL),
        cost_estimate=pl.CostEstimate(flops=10**10, bytes_accessed=4 * 10**6, transcendentals=10**7),
        name="last_section",
    )(steps, *args)


def shards(
    text_states,
    token_ids,
    step_ids,
    base_noise,
    upscale_noise,
    final_noise,
    t5_gain,
    base_keyval,
    upscale_keyval,
    base_input,
    base_time,
    base_gain,
    base_conv,
    base_query,
    base_output,
    base_head,
    upscale_input,
    upscale_time,
    upscale_gain,
    upscale_conv,
    upscale_query,
    upscale_output,
    upscale_head,
):
    groups = lax.axis_size("space")
    segments = lax.axis_size("segment")
    ratio = groups // segments
    micro, _, ltxt, dt5 = text_states.shape
    rows_dev, cols = final_noise.shape[3:]
    tall = rows_dev * groups // cols

    noise_t = final_noise.swapaxes(3, 4)
    swaps = [(i, i + 1) for i in range(0, groups - 1, 2)]
    near = lax.ppermute(noise_t, "space", swaps + [(j, i) for i, j in swaps])
    swaps = [(i, i + 1) for i in range(1, groups - 1, 2)]
    far = lax.ppermute(noise_t, "space", swaps + [(j, i) for i, j in swaps])

    steps = step_ids.T
    chans_base, chans_up = base_query.shape[1], upscale_query.shape[2]
    base_x = base_noise.transpose(1, 2, 0, 3)[0]
    first_x = upscale_noise.transpose(1, 2, 0, 3)[0]
    base_w = (
        base_input,
        base_time,
        base_gain,
        base_conv.reshape(9 * chans_base, chans_base),
        base_query,
        base_output,
        base_head.T,
    )
    up_in = upscale_input.transpose(1, 0, 2)
    up_gain = upscale_gain.transpose(1, 0, 2)
    up_head = upscale_head.transpose(2, 0, 1)
    up_w = (up_in, upscale_time, up_gain, upscale_conv, upscale_query, upscale_output, up_head)
    kv_base, bundle, first_next = front_call(
        segments,
        steps,
        token_ids,
        base_x,
        first_x,
        t5_gain[None],
        base_w,
        up_w,
        text_states.reshape(micro * ltxt, dt5),
        base_keyval,
        upscale_keyval,
    )
    pairs = [
        [
            (s * groups + ratio * q + r, q * groups + ratio * s + (r + k) % ratio)
            for s in range(segments)
            for q in range(segments)
            for r in range(ratio)
        ]
        for k in range(ratio)
    ]
    loads = [lax.ppermute(bundle, ("segment", "space"), pairs[k]) for k in range(ratio)]
    early = base_call(segments, steps, token_ids, base_x, base_w, first_next, kv_base)
    final = last_call(ratio, tall, steps, token_ids, noise_t, near, far, loads, up_w)
    early_states = early.transpose(0, 2, 1, 3)[:, :, None]
    return early_states, final.swapaxes(4, 5)


def solution(mesh):
    placed = (
        P(None, "space", None, None),
        P(),
        P(),
        P(None, "space", None, None),
        P(None, "space", None, None),
        P(None, None, None, "space", None),
    ) + (P(),) * 17
    return jax.shard_map(
        shards,
        mesh=mesh,
        in_specs=placed,
        out_specs=(
            P(None, None, "space", None, "segment"),
            P(None, None, "segment", None, "space", None),
        ),
        check_vma=False,
    )
```

```python
import functools
import math

import jax
import jax.numpy as jnp
from jax import lax
from jax.experimental import pallas as pl
from jax.experimental.pallas import tpu as pltpu
from jax.sharding import PartitionSpec as P


HD = 64
LTXT = 128
VMEM_ALL = 67043328
LOG2E = math.log2(math.e)


NT = (((1,), (1,)), ((), ()))


def unit(x):
    return x * lax.rsqrt(jnp.sum(x * x, axis=-1, keepdims=True) * (1.0 / x.shape[-1]) + 1e-06)


def silu(x):
    return x * (0.5 + 0.5 * jnp.tanh(0.5 * x))


def fdot(a, b):
    return jnp.dot(a, b, preferred_element_type=jnp.float32)


def plane_rows(ref, at, size):
    parts = [ref[c, :, pl.ds(at, size)].astype(jnp.float32) for c in range(ref.shape[0])]
    return jnp.concatenate(parts, axis=0)


def mix_rows(rows, m, micro, total):
    zero = jnp.zeros_like(rows[0])
    out = [row if n == m else zero for row in rows for n in range(micro)]
    if total > len(out):
        out.append(jnp.zeros((total - len(out), rows[0].shape[1]), rows[0].dtype))
    return jnp.concatenate(out, axis=0)


def spread_cols(act, side, pad, dst):
    count, chans = act.shape
    pad[8 : 8 + count] = act
    col = lax.rem(lax.broadcasted_iota(jnp.int32, (count, chans), 0), side)
    left = jnp.where(col == 0, 0.0, pad[7 : 7 + count])
    right = jnp.where(col == side - 1, 0.0, pad[9 : 9 + count])
    dst[:, :chans] = left.astype(jnp.bfloat16)
    dst[:, chans : 2 * chans] = act.astype(jnp.bfloat16)
    dst[:, 2 * chans :] = right.astype(jnp.bfloat16)


def pair_keys(keys, vals):
    first = lax.broadcasted_iota(jnp.int32, keys.shape, 1) < HD
    keys, vals = keys.astype(jnp.float32), vals.astype(jnp.float32)
    kmask = jnp.concatenate([jnp.where(first, keys, 0.0), jnp.where(first, 0.0, keys)], axis=0)
    upper = jnp.concatenate([jnp.where(first, vals, 0.0), jnp.where(first, 1.0, 0.0)], axis=1)
    lower = jnp.concatenate([jnp.where(first, 0.0, vals), jnp.where(first, 0.0, 1.0)], axis=1)
    return kmask.astype(jnp.bfloat16), jnp.concatenate([upper, lower], axis=0).astype(jnp.bfloat16)


def attend_pair(query, kmask, vaug, bias):
    lanes = query.shape[1]
    half = kmask.shape[0] // 2
    scores = lax.dot_general(query, kmask, NT, preferred_element_type=jnp.float32) + bias
    probs = []
    for e in range(2):
        part = scores[:, e * half : (e + 1) * half]
        probs.append(jnp.exp2(part - jnp.max(part, axis=-1, keepdims=True)).astype(jnp.bfloat16))
    both = fdot(jnp.concatenate(probs, axis=1), vaug)
    return (both[:, :lanes] / both[:, lanes:]).astype(jnp.bfloat16)


def key_bias(ids_ref, m, who):
    bias = jnp.where(ids_ref[m, pl.ds(who, 1)] == 0, -1e30, 0.0)
    return jnp.concatenate([bias, bias], axis=1)


def back_part(h1, micro, keyvals, biases, gain1, gain2, w_query, w_out, head_rows):
    count, width = h1.shape
    each = count // micro
    query = fdot((unit(h1) * gain1).astype(jnp.bfloat16), w_query)
    query = (query * (HD**-0.5 * LOG2E)).astype(jnp.bfloat16)
    mixed = []
    for m in range(micro):
        cols = []
        for g in range(width // (2 * HD)):
            at = slice(2 * HD * g, 2 * HD * (g + 1))
            kmask, vaug = pair_keys(keyvals[m](at), keyvals[m](slice(width + at.start, width + at.stop)))
            cols.append(attend_pair(query[m * each : (m + 1) * each, at], kmask, vaug, biases[m]))
        mixed.append(jnp.concatenate(cols, axis=1) if len(cols) > 1 else cols[0])
    h2 = h1 + fdot(jnp.concatenate(mixed, axis=0), w_out)
    normed = (unit(h2) * gain2).astype(jnp.bfloat16)
    eps = 0.0
    for m in range(micro):
        rows = mix_rows(head_rows, m, micro, 16).astype(jnp.bfloat16)
        eps = eps + lax.dot_general(
            rows, normed[m * each : (m + 1) * each], NT, preferred_element_type=jnp.float32
        )
    return eps[: 3 * micro]


def alpha_bar(step):
    frac = (step / 1000.0 + 0.008) / 1.008
    return jnp.cos(frac * (math.pi / 2)) ** 2


def embed(step_ref, sec, chans):
    lane = lax.broadcasted_iota(jnp.int32, (16, chans), 1)
    row = lax.broadcasted_iota(jnp.int32, (16, chans), 0)
    half = chans // 2
    steps = jnp.zeros((16, chans), jnp.float32)
    for m in range(step_ref.shape[0]):
        steps = jnp.where(row == m, step_ref[m, sec].astype(jnp.float32), steps)
    angle = steps * jnp.exp(lax.rem(lane, half).astype(jnp.float32) * (-math.log(10000.0) / half))
    return jnp.where(lane < half, jnp.sin(angle), jnp.cos(angle)).astype(jnp.bfloat16)


def levels(step_ref, m, sec):
    step = jnp.full((8, 128), step_ref[m, sec].astype(jnp.float32))
    level, earlier = alpha_bar(step), alpha_bar(step - 50.0)
    out = (jnp.sqrt(1.0 - level), 1.0 / jnp.sqrt(level), jnp.sqrt(earlier), jnp.sqrt(1.0 - earlier))
    return [part[:1, :1] for part in out]


def denoise(noise, eps, step_ref, sec):
    micro = step_ref.shape[0]
    which = lax.rem(lax.broadcasted_iota(jnp.int32, eps.shape, 0), micro)
    table = [levels(step_ref, m, sec) for m in range(micro)]

    def scalar(n):
        out = jnp.broadcast_to(table[0][n], eps.shape)
        for m in range(1, micro):
            out = jnp.where(which == m, table[m][n], out)
        return out

    clean = jnp.clip((noise - scalar(0) * eps) * scalar(1), -1.0, 1.0)
    return clean, scalar(2) * clean + scalar(3) * eps


def begin(pairs, sems):
    copies = [pltpu.make_async_copy(src, dst, sems.at[n]) for n, (src, dst) in enumerate(pairs)]
    for copy in copies:
        copy.start()
    return copies


def front_kernel(step_ref, *refs):
    (
        text_hbm,
        t5_hbm,
        ids_hbm,
        base_x_hbm,
        first_x_hbm,
        base_in_hbm,
        base_gain_hbm,
        base_head_hbm,
        up_in_hbm,
        up_gain_hbm,
        up_head_hbm,
        up_time_hbm,
        up_conv_hbm,
        up_query_hbm,
        up_out_hbm,
        time_hbm,
        conv_hbm,
        query_hbm,
        out_hbm,
        kv_base_hbm,
        kv_up_hbm,
    ) = refs[:21]
    kv_base_out, load_out, next_out = refs[21:24]
    (
        text,
        t5_ref,
        ids_ref,
        base_x_ref,
        first_x_ref,
        base_in_ref,
        base_gain_ref,
        base_head_ref,
        up_in_ref,
        up_gain_ref,
        up_head_ref,
        up_time_ref,
        up_conv_ref,
        up_query_ref,
        up_out_ref,
        w_time,
        conv,
        w_query,
        w_out,
        kv_w,
        context,
        scales,
        kv_first,
        pad_base,
        taps,
        wide_x,
        pad_first,
        cols_first,
        sems,
    ) = refs[24:]
    seg, place = lax.axis_index("segment"), lax.axis_index("space")
    segments = lax.axis_size("segment")
    rows_text, dt5 = text.shape
    micro = base_x_ref.shape[1]
    ltxt = rows_text // micro
    cb, cs = base_gain_ref.shape[1], up_gain_ref.shape[2]
    px = base_x_ref.shape[2]
    side = math.isqrt(px)
    quarter = side // 4
    band = side // segments
    bf, f32 = jnp.bfloat16, jnp.float32
    step = kv_w.shape[2]
    half = step // 2
    n_base = kv_base_hbm.shape[1] // step
    chunks = [(kv_base_hbm.at[:, n * step : (n + 1) * step], kv_w.at[n]) for n in range(n_base)]
    chunks += [(kv_up_hbm.at[n], kv_w.at[n_base, :, n * half : (n + 1) * half]) for n in range(2)]
    early = (
        (base_x_hbm, base_x_ref),
        (base_in_hbm, base_in_ref),
        (base_gain_hbm, base_gain_ref),
        (time_hbm, w_time),
        (t5_hbm, t5_ref),
        (text_hbm, text),
    )
    small = (
        (ids_hbm, ids_ref),
        (first_x_hbm, first_x_ref),
        (base_head_hbm, base_head_ref),
        (up_in_hbm, up_in_ref),
        (up_gain_hbm, up_gain_ref),
        (up_head_hbm, up_head_ref),
        (up_time_hbm.at[0], up_time_ref),
        (up_conv_hbm.at[0], up_conv_ref),
        (up_query_hbm.at[0], up_query_ref),
        (up_out_hbm.at[0], up_out_ref),
    )
    late = ((conv_hbm, conv), (query_hbm, w_query), (out_hbm, w_out))
    copies = begin(list(early) + list(small) + chunks + list(late), sems)
    first_small = len(early)
    first_chunk = first_small + len(small)
    after = first_chunk + len(chunks)

    for copy in copies[:4]:
        copy.wait()
    tall = quarter + 1
    temb = fdot(embed(step_ref, 0, cb), w_time[...])
    base_rows = [base_in_ref[c : c + 1].astype(f32) for c in range(3)]
    lanes = 128 * ((tall * side + 127) // 128)
    x_t = jnp.concatenate([plane_rows(base_x_ref, 0, lanes), jnp.zeros((2, lanes), f32)], axis=0)
    x_t = jnp.transpose(x_t)[: tall * side].astype(bf)
    pad_base[: 8 + side] = jnp.zeros((8 + side, cb), f32)
    edge = lax.broadcasted_iota(jnp.int32, (quarter, cb), 0) == 0
    corner_h = []
    for m in range(micro):
        h0 = fdot(x_t, mix_rows(base_rows, m, micro, 8).astype(bf)) + temb[m : m + 1]
        pad_base[8 + side : 8 + side + tall * side] = silu(unit(h0) * base_gain_ref[0:1])
        corner_h.append(
            jnp.concatenate([h0[side * h : side * h + quarter] for h in range(quarter)], axis=0)
        )
        for r in range(quarter + 1):
            for b in range(3):
                lo = pad_base[8 + side * r + b - 1 : 8 + side * r + b - 1 + quarter]
                hi = pad_base[8 + side * (r + 1) + b - 1 : 8 + side * (r + 1) + b - 1 + quarter]
                if b == 0:
                    lo, hi = jnp.where(edge, 0.0, lo), jnp.where(edge, 0.0, hi)
                both = jnp.concatenate([lo, hi], axis=0).astype(bf)
                for a in range(3):
                    h = r - a
                    if h % 2 == 0 and 0 <= h < quarter:
                        at = m * quarter * quarter + h * quarter
                        taps[at : at + 2 * quarter, (3 * a + b) * cb : (3 * a + b + 1) * cb] = both
    copies[4].wait()
    copies[5].wait()
    gain = t5_ref[...]

    def prepare(i, carry):
        at = pl.multiple_of(i * 16, 16)
        x = text[pl.ds(at, 16)].astype(f32)
        scales[pl.ds(at, 16)] = jnp.broadcast_to(
            lax.rsqrt(jnp.sum(x * x, axis=-1, keepdims=True) * (1.0 / dt5) + 1e-06), (16, 128)
        )
        context[pl.ds(at, 16)] = (x * gain).astype(bf)
        return carry

    lax.fori_loop(0, rows_text // 16, prepare, 0)
    for copy in copies[first_small:first_chunk]:
        copy.wait()
    biases = [key_bias(ids_ref, m, place) for m in range(micro)]
    scale = jnp.concatenate([scales[...]] * (step // 128), axis=1)
    for n in range(n_base):
        copies[first_chunk + n].wait()
        kv_base_out[:, n * step : (n + 1) * step] = (fdot(context[...], kv_w[n]) * scale).astype(bf)
    copies[after - 2].wait()
    copies[after - 1].wait()
    copies[after].wait()
    copies[after + 1].wait()
    copies[after + 2].wait()
    h1 = jnp.concatenate(corner_h, axis=0) + fdot(taps[...], conv[...])
    rest_kv = (fdot(context[...], kv_w[n_base]) * scale).astype(bf)
    kv_first[...] = rest_kv[:, :half]
    load_out[: micro * ltxt] = rest_kv[:, half:]
    keyvals = [lambda at, m=m: kv_base_out[m * ltxt : (m + 1) * ltxt, at] for m in range(micro)]
    head_rows = [base_head_ref[c : c + 1].astype(f32) for c in range(3)]
    eps = back_part(
        h1, micro, keyvals, biases, base_gain_ref[1:2], base_gain_ref[2:3], w_query[...], w_out[...], head_rows
    )
    noise = plane_rows(base_x_ref, 0, lanes)
    noise = jnp.concatenate([noise[:, side * h : side * h + quarter] for h in range(quarter)], axis=1)
    corner, _ = denoise(noise, eps, step_ref, 0)

    near = 128 * ((2 * side + 127) // 128)
    window = near + band * side + near
    wide_x[...] = jnp.zeros_like(wide_x)
    wide_x[: 3 * micro, near : near + px] = plane_rows(first_x_ref, 0, px)
    x_win = wide_x[:, pl.ds(pl.multiple_of(seg * (band * side), 128), window)]
    spot = lax.broadcasted_iota(jnp.int32, (quarter * quarter, window), 0)
    pixel = lax.broadcasted_iota(jnp.int32, (quarter * quarter, window), 1) + (seg * band * side - near)
    rise = side // quarter
    hit = (lax.shift_right_arithmetic(pixel, (side * rise).bit_length() - 1) == lax.div(spot, quarter)) & (
        lax.div(lax.rem(pixel + 4 * px, side), rise) == lax.rem(spot, quarter)
    )
    corner16 = jnp.concatenate([corner, jnp.zeros((16 - 3 * micro, corner.shape[1]), f32)], axis=0).astype(bf)
    cond = fdot(corner16, jnp.where(hit, 1.0, 0.0).astype(bf))[:8]
    x_t = jnp.transpose(jnp.concatenate([x_win, cond], axis=0))
    skip = near - 2 * side
    total = (band + 4) * side
    x_t = x_t[skip : skip + total].astype(bf)
    temb = fdot(embed(step_ref, 1, cs), up_time_ref[...])
    up_rows = [up_in_ref[c, 0:1].astype(f32) for c in range(6)]
    row = lax.div(lax.broadcasted_iota(jnp.int32, (total, cs), 0), side) + (seg * band - 2)
    inside = (row >= 0) & (row < side)
    kept = (band + 2) * side
    first_h, lhs = [], []
    for m in range(micro):
        rhs = jnp.concatenate(
            [mix_rows(up_rows[:3], m, micro, 8), mix_rows(up_rows[3:], m, micro, 8)], axis=0
        ).astype(bf)
        h0 = fdot(x_t, rhs) + temb[m : m + 1]
        act = jnp.where(inside, silu(unit(h0) * up_gain_ref[0, 0:1]), 0.0)
        spread_cols(act, side, pad_first, cols_first.at[m])
        first_h.append(h0[side : side + kept])
        lhs.append(
            jnp.concatenate([cols_first[m, a * side : a * side + kept] for a in range(3)], axis=1)
        )
    h1 = jnp.concatenate(first_h, axis=0) + fdot(jnp.concatenate(lhs, axis=0), up_conv_ref[...].reshape(9 * cs, cs))
    keyvals = [lambda at, m=m: kv_first[m * ltxt : (m + 1) * ltxt, at] for m in range(micro)]
    head_rows = [up_head_ref[c, 0:1].astype(f32) for c in range(3)]
    eps = back_part(
        h1, micro, keyvals, biases, up_gain_ref[1, 0:1], up_gain_ref[2, 0:1], up_query_ref[...], up_out_ref[...],
        head_rows,
    )
    noise = x_win[: 3 * micro, near - side : near - side + kept]
    clean, prior = denoise(noise, eps, step_ref, 1)
    for c in range(3):
        next_out[c] = prior[c * micro : (c + 1) * micro, side : side + band * side].astype(bf)
    wide = load_out.shape[1]
    blocks = (load_out.shape[0] - micro * ltxt) // 16
    clean = jnp.concatenate([clean, jnp.zeros((3 * micro, blocks * wide - kept), f32)], axis=1)
    clean = jnp.concatenate([clean, jnp.zeros((16 - 3 * micro, blocks * wide), f32)], axis=0).astype(bf)
    for b in range(blocks):
        at = micro * ltxt + 16 * b
        load_out[at : at + 16] = clean[:, b * wide : (b + 1) * wide]


def base_kernel(step_ref, *refs):
    hbm, early_ref, vmem, extra = refs[:11], refs[11], refs[12:23], refs[23:]
    x_ref, w_in_ref, gain_ref, head_ref, time_ref, ids_ref, next_ref, kv_ref, conv, w_query, w_out = vmem
    wide_x, pad, cols, sems = extra
    seg, place = lax.axis_index("segment"), lax.axis_index("space")
    segments = lax.axis_size("segment")
    micro, px = x_ref.shape[1:]
    side = math.isqrt(px)
    band = side // segments
    ltxt = kv_ref.shape[0] // micro
    bf, f32 = jnp.bfloat16, jnp.float32
    copies = begin(list(zip(hbm, vmem)), sems)
    for copy in copies[:5]:
        copy.wait()
    chans = gain_ref.shape[1]
    near = 128 * ((side + 127) // 128)
    window = near + band * side + near
    wide_x[...] = jnp.zeros_like(wide_x)
    wide_x[: 3 * micro, near : near + px] = plane_rows(x_ref, 0, px)
    x_win = wide_x[:, pl.ds(pl.multiple_of(seg * (band * side), 128), window)]
    total = (band + 2) * side
    x_t = jnp.transpose(x_win)[near - side : near - side + total].astype(bf)
    temb = fdot(embed(step_ref, 0, chans), time_ref[...])
    rows = [w_in_ref[c : c + 1].astype(f32) for c in range(3)]
    row = lax.div(lax.broadcasted_iota(jnp.int32, (total, chans), 0), side) + (seg * band - 1)
    inside = (row >= 0) & (row < side)
    kept = band * side
    hid, lhs = [], []
    for m in range(micro):
        h0 = fdot(x_t, mix_rows(rows, m, micro, 8).astype(bf)) + temb[m : m + 1]
        act = jnp.where(inside, silu(unit(h0) * gain_ref[0:1]), 0.0)
        spread_cols(act, side, pad, cols.at[m])
        hid.append(h0[side : side + kept])
        lhs.append(jnp.concatenate([cols[m, a * side : a * side + kept] for a in range(3)], axis=1))
    for copy in copies[5:9]:
        copy.wait()
    h1 = jnp.concatenate(hid, axis=0) + fdot(jnp.concatenate(lhs, axis=0), conv[...])
    copies[9].wait()
    copies[10].wait()
    biases = [key_bias(ids_ref, m, place) for m in range(micro)]
    keyvals = [lambda at, m=m: kv_ref[m * ltxt : (m + 1) * ltxt, at] for m in range(micro)]
    head_rows = [head_ref[c : c + 1].astype(f32) for c in range(3)]
    eps = back_part(
        h1, micro, keyvals, biases, gain_ref[1:2], gain_ref[2:3], w_query[...], w_out[...], head_rows
    )
    _, prior = denoise(x_win[: 3 * micro, near : near + kept], eps, step_ref, 0)
    for c in range(3):
        early_ref[0, c] = prior[c * micro : (c + 1) * micro].astype(bf)
    early_ref[1] = next_ref[...]


def like(array, index=None):
    shape = array.shape if index is None else array.shape[1:]
    return pltpu.VMEM(shape, array.dtype)


def front_call(segments, steps, ids, base_x, first_x, t5, base_w, up_w, text, kv_base_w, kv_up_w):
    base_in, base_time, base_gain, base_conv, base_query, base_output, base_head = base_w
    up_in, up_time, up_gain, up_conv, up_query, up_out, up_head = up_w
    rows_text, dt5 = text.shape
    micro, px = base_x.shape[1:]
    side = math.isqrt(px)
    band = side // segments
    quarter = side // 4
    cb, cs = base_gain.shape[1], up_gain.shape[2]
    step = kv_up_w.shape[2]
    chunks = kv_base_w.shape[1] // step + 2
    near = 128 * ((2 * side + 127) // 128)
    blocks = -(-((band + 2) * side) // step)
    bf, f32 = jnp.bfloat16, jnp.float32
    smem = pl.BlockSpec(memory_space=pltpu.SMEM)
    vmem = pl.BlockSpec(memory_space=pltpu.VMEM)
    hbm = pl.BlockSpec(memory_space=pltpu.HBM)
    whole = (text, t5, ids, base_x, first_x, base_in, base_gain, base_head, up_in, up_gain, up_head)
    cut = (up_time, up_conv, up_query, up_out)
    big = (base_time, base_conv, base_query, base_output)
    args = whole + cut + big + (kv_base_w, kv_up_w)
    return pl.pallas_call(
        front_kernel,
        out_shape=(
            jax.ShapeDtypeStruct((rows_text, 2 * cb), bf),
            jax.ShapeDtypeStruct((rows_text + 16 * blocks, step), bf),
            jax.ShapeDtypeStruct((3, micro, band * side), bf),
        ),
        in_specs=[smem] + [hbm] * len(args),
        out_specs=(vmem, vmem, vmem),
        scratch_shapes=[like(a) for a in whole]
        + [like(a, 0) for a in cut]
        + [like(a) for a in big]
        + [
            pltpu.VMEM((chunks // 2, dt5, 2 * step), bf),
            pltpu.VMEM((rows_text, dt5), bf),
            pltpu.VMEM((rows_text, 128), f32),
            pltpu.VMEM((rows_text, step), bf),
            pltpu.VMEM((16 + side + (quarter + 1) * side, cb), f32),
            pltpu.VMEM((micro * quarter * quarter, 9 * cb), bf),
            pltpu.VMEM((8, near + px + near), f32),
            pltpu.VMEM(((band + 4) * side + 16, cs), f32),
            pltpu.VMEM((micro, (band + 4) * side, 3 * cs), bf),
            pltpu.SemaphoreType.DMA((chunks + 19,)),
        ],
        compiler_params=pltpu.CompilerParams(vmem_limit_bytes=VMEM_ALL),
        cost_estimate=pl.CostEstimate(flops=5 * 10**9, bytes_accessed=22 * 10**6, transcendentals=10**6),
        name="text_and_first",
    )(steps, *args)


def base_call(segments, steps, ids, base_x, base_w, first_next, kv_base):
    base_in, base_time, base_gain, base_conv, base_query, base_output, base_head = base_w
    micro, px = base_x.shape[1:]
    side = math.isqrt(px)
    band = side // segments
    cb = base_gain.shape[1]
    near = 128 * ((side + 127) // 128)
    bf, f32 = jnp.bfloat16, jnp.float32
    smem = pl.BlockSpec(memory_space=pltpu.SMEM)
    vmem = pl.BlockSpec(memory_space=pltpu.VMEM)
    hbm = pl.BlockSpec(memory_space=pltpu.HBM)
    args = (base_x, base_in, base_gain, base_head, base_time, ids, first_next, kv_base, base_conv, base_query)
    args += (base_output,)
    return pl.pallas_call(
        base_kernel,
        out_shape=jax.ShapeDtypeStruct((2, 3, micro, band * side), bf),
        in_specs=[smem] + [hbm] * len(args),
        out_specs=vmem,
        scratch_shapes=[like(a) for a in args]
        + [
            pltpu.VMEM((8, near + px + near), f32),
            pltpu.VMEM(((band + 2) * side + 16, cb), f32),
            pltpu.VMEM((micro, (band + 2) * side, 3 * cb), bf),
            pltpu.SemaphoreType.DMA((len(args),)),
        ],
        compiler_params=pltpu.CompilerParams(vmem_limit_bytes=VMEM_ALL),
        cost_estimate=pl.CostEstimate(flops=4 * 10**9, bytes_accessed=7 * 10**6, transcendentals=10**6),
        name="base_section",
    )(steps, *args)


def last_kernel(ratio, tall, step_ref, *refs):
    hbm, out_ref = refs[: 11 + ratio], refs[11 + ratio]
    ids_ref, mine_ref, near_ref, far_ref, w_in_ref, gain_ref, head_ref, w_time_ref, conv_ref, query_ref, out_w_ref = refs[
        12 + ratio : 23 + ratio
    ]
    load, inbig, headbig, wpair, wq2, wo2, cond_pick, act, turn, *halves, sems = refs[23 + ratio :]
    slots = (halves[:3], halves[3:])
    seg, place = lax.axis_index("segment"), lax.axis_index("space")
    groups = lax.axis_size("space")
    micro = step_ref.shape[0]
    span = load.shape[1] - micro * LTXT
    own = pl.ds(seg * ratio, ratio)
    pairs_io = [(hbm[4], w_in_ref), (hbm[5], gain_ref), (hbm[6], head_ref)]
    pairs_io += [(hbm[7 + n].at[1], ref) for n, ref in enumerate((w_time_ref, conv_ref, query_ref, out_w_ref))]
    pairs_io += [(hbm[0], ids_ref)]
    pairs_io += [(hbm[1 + n].at[:, own], ref) for n, ref in enumerate((mine_ref, near_ref, far_ref))]
    pairs_io += [(hbm[11 + k], load.at[k]) for k in range(ratio)]
    copies = begin(pairs_io, sems)
    chans = query_ref.shape[0]
    wide, high = mine_ref.shape[3:]
    ltxt = LTXT
    planes = 3 * wide
    phase = lax.rem(place, ratio)
    odd_place = lax.rem(place, 2) == 1
    cond_dev = high // tall
    pairs = wide // 2
    rows = high + 16
    lane2 = 2 * chans

    for copy in copies[:7]:
        copy.wait()
    row_id = lax.broadcasted_iota(jnp.int32, (2 * planes, chans), 0)
    stack = jnp.concatenate(
        [jnp.broadcast_to(w_in_ref[c, 1:2].astype(jnp.float32), (wide, chans)) for c in range(6)], axis=0
    )
    heads3 = jnp.concatenate(
        [jnp.broadcast_to(head_ref[c, 1:2].astype(jnp.float32), (wide, chans)) for c in range(3)], axis=0
    )
    for w in range(wide):
        here = lax.rem(row_id, wide) == w
        inbig[:, w * chans : (w + 1) * chans] = jnp.where(here, stack, 0.0).astype(jnp.bfloat16)
        headbig[:, w * chans : (w + 1) * chans] = jnp.where(here[:planes], heads3, 0.0).astype(jnp.bfloat16)
    zero_tap = jnp.zeros((chans, chans), jnp.bfloat16)
    for d in range(4):
        for a in range(3):
            at = (d * 3 + a) * chans
            wpair[at : at + chans, :chans] = conv_ref[3 * a + d] if d < 3 else zero_tap
            wpair[at : at + chans, chans:] = conv_ref[3 * a + d - 1] if d > 0 else zero_tap
    for dst, src in ((wq2, query_ref), (wo2, out_w_ref)):
        dst[:chans, :chans] = src[...]
        dst[:chans, chans:] = zero_tap
        dst[chans:, :chans] = zero_tap
        dst[chans:, chans:] = src[...]
    strip = cond_pick.shape[0] // 3
    pick_row = lax.broadcasted_iota(jnp.int32, (strip, planes), 0)
    pick_lane = lax.broadcasted_iota(jnp.int32, (strip, planes), 1)
    for c in range(3):
        hit = (pick_lane == c * wide + lax.rem(pick_row, wide))
        cond_pick[c * strip : (c + 1) * strip] = jnp.where(hit, 1.0, 0.0).astype(jnp.bfloat16)
    turn[...] = jnp.zeros_like(turn)
    for even, odd, _ in slots:
        even[0] = jnp.zeros(even.shape[1:], even.dtype)
        odd[pairs] = jnp.zeros(odd.shape[1:], odd.dtype)

    temb = fdot(embed(step_ref, 2, chans), w_time_ref[...])
    top_ok = jnp.where(place > 0, 1.0, 0.0)
    low_ok = jnp.where(place < groups - 1, 1.0, 0.0)
    gain0, gain1, gain2 = gain_ref[0, 1:2], gain_ref[1, 1:2], gain_ref[2, 1:2]
    inv = 1.0 / chans

    tile = lambda n: lax.div(lax.broadcasted_iota(jnp.int32, (lane2, lane2), n), chans)
    ones2 = jnp.where(tile(0) == tile(1), 1.0, 0.0).astype(jnp.bfloat16)
    gain0, gain1, gain2 = (jnp.concatenate([g, g], axis=1) for g in (gain0, gain1, gain2))

    def norm(x):
        total = fdot((x * x).astype(jnp.bfloat16), ones2)
        return x * lax.rsqrt(total * inv + 1e-06)

    tables = [levels(step_ref, m, 2) for m in range(micro)]
    for copy in copies[7:]:
        copy.wait()

    def lane_norm(x):
        return x * lax.rsqrt(jnp.sum(x * x, axis=-1, keepdims=True) * inv + 1e-06)

    duos = ratio // 2

    def spot(i):
        m, k = lax.div(i, ratio), lax.rem(i, ratio)
        duo = lax.rem(lax.div(phase, 2) - lax.rem(k, duos) + duos, duos)
        return m, k, 2 * duo + lax.rem(phase + lax.div(k, duos), 2)

    def front(i, slot):
        even, odd, hid = slots[slot]
        m, k, r = spot(i)
        temb_m = jnp.where(m == 0, temb[0:1], temb[1:2])
        temb2 = jnp.concatenate([temb_m, temb_m], axis=1)

        def window(ref, n):
            turn[n, :planes, :high] = ref[m, r].reshape(planes, high).astype(jnp.float32)
            return jnp.transpose(turn[n])

        body = window(mine_ref, 0)[:high, :planes]
        near = window(near_ref, 1)
        far = window(far_ref, 2)
        top = jnp.where(odd_place, near[high - 1 : high, :planes], far[high - 1 : high, :planes])
        low = jnp.where(odd_place, far[0:1, :planes], near[0:1, :planes])
        noise_rows = jnp.concatenate([body, top, low, jnp.zeros((14, planes), jnp.float32)], axis=0)
        blocks = [
            load[k, micro * ltxt + 16 * b : micro * ltxt + 16 * b + 8].astype(jnp.float32) for b in range(span // 16)
        ]
        band_planes = jnp.concatenate(blocks, axis=1)[:, :strip]
        row_h = lax.broadcasted_iota(jnp.int32, (rows, strip), 0)
        lane_px = lax.broadcasted_iota(jnp.int32, (rows, strip), 1)
        need = jnp.where(row_h < high, 1 + lax.div(row_h, tall), jnp.where(row_h == high, 0, cond_dev + 1))
        hit = lax.div(lane_px, wide) == need + phase * cond_dev
        spread = []
        for c in range(3):
            plane = jnp.where(m == 0, band_planes[2 * c : 2 * c + 1], band_planes[2 * c + 1 : 2 * c + 2])
            spread.append(jnp.where(hit, jnp.broadcast_to(plane, (rows, strip)), 0.0).astype(jnp.bfloat16))
        cond_rows = fdot(jnp.concatenate(spread, axis=1), cond_pick[...])
        pixels = jnp.concatenate([noise_rows, cond_rows], axis=1).astype(jnp.bfloat16)
        yield

        for t in range(pairs):
            h0 = fdot(pixels, inbig[:, t * lane2 : (t + 1) * lane2]) + temb2
            hid[t] = h0[:high]
            for par in range(2):
                x = silu(lane_norm(h0[:, par * chans : (par + 1) * chans]) * gain0[:, :chans])
                at = (t % 4) * 2 + par
                act[at, 8 : 8 + high] = x[:high]
                act[at, 7:8] = x[high : high + 1] * top_ok
                act[at, 8 + high : 9 + high] = x[high + 1 : high + 2] * low_ok
                wide3 = jnp.concatenate(
                    [act[at, 7 + a : 7 + a + high].astype(jnp.bfloat16) for a in range(3)], axis=1
                )
                if par == 0:
                    odd[t] = wide3
                else:
                    even[t + 1] = wide3
            if t % 2:
                yield

    subs = 2
    each = pairs // subs
    m_rows = each * high

    def back(i, slot):
        even, odd, hid = slots[slot]
        m, k, r = spot(i)
        keys = load[k, pl.ds(pl.multiple_of(m * ltxt, ltxt), ltxt), :chans]
        vals = load[k, pl.ds(pl.multiple_of(m * ltxt, ltxt), ltxt), chans:]
        kmask, vaug = pair_keys(keys, vals)
        bias = key_bias(ids_ref, m, seg * ratio + r)
        h1, mx = [], []
        for n in range(subs):
            at = n * each
            parts = (even[at : at + each], odd[at : at + each], even[at + 1 : at + 1 + each], odd[at + 1 : at + 1 + each])
            lhs = jnp.concatenate([part.reshape(m_rows, 3 * chans) for part in parts], axis=1)
            h1.append(fdot(lhs, wpair[...]) + hid[at : at + each].reshape(m_rows, lane2))
            yield
        query = []
        for n in range(subs):
            qn = fdot((norm(h1[n]) * gain1).astype(jnp.bfloat16), wq2[...])
            query.append((qn * (HD**-0.5 * LOG2E)).astype(jnp.bfloat16))
        yield
        for n in range(subs):
            mixed = []
            for p in range(2):
                mixed.append(attend_pair(query[n][:, p * chans : (p + 1) * chans], kmask, vaug, bias))
                yield
            mx.append(jnp.concatenate(mixed, axis=1))
        eps = jnp.zeros((planes, high), jnp.float32)
        for n in range(subs):
            h2 = h1[n] + fdot(mx[n], wo2[...])
            rows2 = (norm(h2) * gain2).astype(jnp.bfloat16).reshape(each, high, lane2)
            rows2 = jnp.concatenate([rows2[u] for u in range(each)], axis=1)
            eps = eps + lax.dot_general(
                headbig[:, n * each * lane2 : (n + 1) * each * lane2], rows2, NT, preferred_element_type=jnp.float32
            )
            yield
        noise = mine_ref[m, r].reshape(planes, high).astype(jnp.float32)
        ca, cb, cc, cd = (jnp.where(m == 0, tables[0][n], tables[1][n]) for n in range(4))
        clean = jnp.clip((noise - ca * eps) * cb, -1.0, 1.0)
        prior = cc * clean + cd * eps
        out_ref[0, m, r] = clean.astype(jnp.bfloat16).reshape(3, wide, high)
        out_ref[1, m, r] = prior.astype(jnp.bfloat16).reshape(3, wide, high)

    def together(*streams):
        live = list(streams)
        while live:
            live = [stream for stream in live if next(stream, stop) is not stop]

    stop = object()
    total = micro * ratio

    def couple(j, carry):
        together(back(2 * j, 0), front(2 * j + 1, 1))
        together(back(2 * j + 1, 1), front(jnp.minimum(2 * j + 2, total - 1), 0))
        return carry

    together(front(0, 0))
    lax.fori_loop(0, total // 2, couple, 0)


def last_call(ratio, tall, steps, ids, noise, near, far, loads, weights):
    w_in, w_time, gains, w_conv, w_query, w_out, head = weights
    micro, _, _, wide, high = noise.shape
    chans = w_query.shape[1]
    planes = 3 * wide
    pairs = wide // 2
    strip = 512
    smem = pl.BlockSpec(memory_space=pltpu.SMEM)
    vmem = pl.BlockSpec(memory_space=pltpu.VMEM)
    hbm = pl.BlockSpec(memory_space=pltpu.HBM)
    bf, f32 = jnp.bfloat16, jnp.float32
    args = (ids, noise, near, far, w_in, gains, head, w_time, w_conv, w_query, w_out) + tuple(loads)
    part = pltpu.VMEM((micro, ratio, 3, wide, high), bf)
    return pl.pallas_call(
        functools.partial(last_kernel, ratio, tall),
        out_shape=jax.ShapeDtypeStruct((2, micro, ratio, 3, wide, high), bf),
        in_specs=[smem] + [hbm] * len(args),
        out_specs=vmem,
        scratch_shapes=[like(ids), part, part, part, like(w_in), like(gains), like(head)]
        + [like(a, 0) for a in (w_time, w_conv, w_query, w_out)]
        + [
            pltpu.VMEM((ratio,) + loads[0].shape, bf),
            pltpu.VMEM((2 * planes, wide * chans), bf),
            pltpu.VMEM((planes, wide * chans), bf),
            pltpu.VMEM((12 * chans, 2 * chans), bf),
            pltpu.VMEM((2 * chans, 2 * chans), bf),
            pltpu.VMEM((2 * chans, 2 * chans), bf),
            pltpu.VMEM((3 * strip, planes), bf),
            pltpu.VMEM((8, high + 16, chans), f32),
            pltpu.VMEM((3, 128, 128), f32),
        ]
        + [
            pltpu.VMEM((pairs + 1, high, 3 * chans), bf),
            pltpu.VMEM((pairs + 1, high, 3 * chans), bf),
            pltpu.VMEM((pairs, high, 2 * chans), f32),
        ]
        * 2
        + [
            pltpu.SemaphoreType.DMA((len(args),)),
        ],
        compiler_params=pltpu.CompilerParams(vmem_limit_bytes=VMEM_ALL),
        cost_estimate=pl.CostEstimate(flops=10**10, bytes_accessed=4 * 10**6, transcendentals=10**7),
        name="last_section",
    )(steps, *args)


def shards(
    text_states,
    token_ids,
    step_ids,
    base_noise,
    upscale_noise,
    final_noise,
    t5_gain,
    base_keyval,
    upscale_keyval,
    base_input,
    base_time,
    base_gain,
    base_conv,
    base_query,
    base_output,
    base_head,
    upscale_input,
    upscale_time,
    upscale_gain,
    upscale_conv,
    upscale_query,
    upscale_output,
    upscale_head,
):
    groups = lax.axis_size("space")
    segments = lax.axis_size("segment")
    ratio = groups // segments
    micro, _, ltxt, dt5 = text_states.shape
    rows_dev, cols = final_noise.shape[3:]
    tall = rows_dev * groups // cols

    noise_t = final_noise.swapaxes(3, 4)
    swaps = [(i, i + 1) for i in range(0, groups - 1, 2)]
    near = lax.ppermute(noise_t, "space", swaps + [(j, i) for i, j in swaps])
    swaps = [(i, i + 1) for i in range(1, groups - 1, 2)]
    far = lax.ppermute(noise_t, "space", swaps + [(j, i) for i, j in swaps])

    steps = step_ids.T
    chans_base = base_query.shape[1]
    base_x = base_noise.transpose(1, 2, 0, 3)[0]
    first_x = upscale_noise.transpose(1, 2, 0, 3)[0]
    base_w = (
        base_input,
        base_time,
        base_gain,
        base_conv.reshape(9 * chans_base, chans_base),
        base_query,
        base_output,
        base_head.T,
    )
    up_in = upscale_input.transpose(1, 0, 2)
    up_gain = upscale_gain.transpose(1, 0, 2)
    up_head = upscale_head.transpose(2, 0, 1)
    up_w = (up_in, upscale_time, up_gain, upscale_conv, upscale_query, upscale_output, up_head)
    kv_base, bundle, first_next = front_call(
        segments,
        steps,
        token_ids,
        base_x,
        first_x,
        t5_gain[None],
        base_w,
        up_w,
        text_states.reshape(micro * ltxt, dt5),
        base_keyval,
        upscale_keyval,
    )
    duos = ratio // 2
    cross = [
        [
            (s * groups + ratio * q + r, q * groups + ratio * s + 2 * ((r // 2 + k) % duos) + r % 2)
            for s in range(segments)
            for q in range(segments)
            for r in range(ratio)
        ]
        for k in range(duos)
    ]
    got = [lax.ppermute(bundle, ("segment", "space"), cross[k]) for k in range(duos)]
    early = base_call(segments, steps, token_ids, base_x, base_w, first_next, kv_base)
    mates = [(i, i ^ 1) for i in range(groups)]
    got, early = lax.optimization_barrier((got, early))
    loads = got + [lax.ppermute(array, "space", mates) for array in got]
    final = last_call(ratio, tall, steps, token_ids, noise_t, near, far, loads, up_w)
    early_states = early.transpose(0, 2, 1, 3)[:, :, None]
    return early_states, final.swapaxes(4, 5)


def solution(mesh):
    placed = (
        P(None, "space", None, None),
        P(),
        P(),
        P(None, "space", None, None),
        P(None, "space", None, None),
        P(None, None, None, "space", None),
    ) + (P(),) * 17

    return jax.shard_map(
        shards,
        mesh=mesh,
        in_specs=placed,
        out_specs=(
            P(None, None, "space", None, "segment"),
            P(None, None, "segment", None, "space", None),
        ),
        check_vma=False,
    )
```

```python
import functools
import math

import jax
import jax.numpy as jnp
from jax import lax
from jax.experimental import pallas as pl
from jax.experimental.pallas import tpu as pltpu
from jax.sharding import PartitionSpec as P


HD = 64
LTXT = 128
VMEM_ALL = 67043328
LOG2E = math.log2(math.e)


NT = (((1,), (1,)), ((), ()))


def unit(x):
    return x * lax.rsqrt(jnp.sum(x * x, axis=-1, keepdims=True) * (1.0 / x.shape[-1]) + 1e-06)


def silu(x):
    return x * (0.5 + 0.5 * jnp.tanh(0.5 * x))


def fdot(a, b):
    return jnp.dot(a, b, preferred_element_type=jnp.float32)


def plane_rows(ref, at, size):
    parts = [ref[c, :, pl.ds(at, size)].astype(jnp.float32) for c in range(ref.shape[0])]
    return jnp.concatenate(parts, axis=0)


def mix_rows(rows, m, micro, total):
    zero = jnp.zeros_like(rows[0])
    out = [row if n == m else zero for row in rows for n in range(micro)]
    if total > len(out):
        out.append(jnp.zeros((total - len(out), rows[0].shape[1]), rows[0].dtype))
    return jnp.concatenate(out, axis=0)


def spread_cols(act, side, pad, dst):
    count, chans = act.shape
    pad[8 : 8 + count] = act
    col = lax.broadcasted_iota(jnp.int32, (1, side, chans), 1)
    left = pad[7 : 7 + count].reshape(count // side, side, chans)
    right = pad[9 : 9 + count].reshape(count // side, side, chans)
    left = jnp.where(col == 0, 0.0, left).reshape(count, chans)
    right = jnp.where(col == side - 1, 0.0, right).reshape(count, chans)
    dst[:, :chans] = left.astype(jnp.bfloat16)
    dst[:, chans : 2 * chans] = act.astype(jnp.bfloat16)
    dst[:, 2 * chans :] = right.astype(jnp.bfloat16)


def inside_only(act, outer, seg, segments):
    top = act[:outer] * jnp.where(seg > 0, 1.0, 0.0)
    low = act[act.shape[0] - outer :] * jnp.where(seg < segments - 1, 1.0, 0.0)
    return jnp.concatenate([top, act[outer : act.shape[0] - outer], low], axis=0)


def pair_keys(keys, vals):
    first = lax.broadcasted_iota(jnp.int32, keys.shape, 1) < HD
    keys, vals = keys.astype(jnp.float32), vals.astype(jnp.float32)
    kmask = jnp.concatenate([jnp.where(first, keys, 0.0), jnp.where(first, 0.0, keys)], axis=0)
    upper = jnp.concatenate([jnp.where(first, vals, 0.0), jnp.where(first, 1.0, 0.0)], axis=1)
    lower = jnp.concatenate([jnp.where(first, 0.0, vals), jnp.where(first, 0.0, 1.0)], axis=1)
    return kmask.astype(jnp.bfloat16), jnp.concatenate([upper, lower], axis=0).astype(jnp.bfloat16)


def attend_pair(query, kmask, vaug, bias):
    lanes = query.shape[1]
    half = kmask.shape[0] // 2
    scores = lax.dot_general(query, kmask, NT, preferred_element_type=jnp.float32) + bias
    probs = []
    for e in range(2):
        part = scores[:, e * half : (e + 1) * half]
        probs.append(jnp.exp2(part - jnp.max(part, axis=-1, keepdims=True)).astype(jnp.bfloat16))
    both = fdot(jnp.concatenate(probs, axis=1), vaug)
    return (both[:, :lanes] / both[:, lanes:]).astype(jnp.bfloat16)


def key_bias(ids_ref, m, who):
    bias = jnp.where(ids_ref[m, pl.ds(who, 1)] == 0, -1e30, 0.0)
    return jnp.concatenate([bias, bias], axis=1)


def back_part(h1, micro, keyvals, biases, gain1, gain2, w_query, w_out, head_rows):
    count, width = h1.shape
    each = count // micro
    query = fdot((unit(h1) * gain1).astype(jnp.bfloat16), w_query)
    query = (query * (HD**-0.5 * LOG2E)).astype(jnp.bfloat16)
    mixed = []
    for m in range(micro):
        cols = []
        for g in range(width // (2 * HD)):
            at = slice(2 * HD * g, 2 * HD * (g + 1))
            kmask, vaug = pair_keys(keyvals[m](at), keyvals[m](slice(width + at.start, width + at.stop)))
            cols.append(attend_pair(query[m * each : (m + 1) * each, at], kmask, vaug, biases[m]))
        mixed.append(jnp.concatenate(cols, axis=1) if len(cols) > 1 else cols[0])
    h2 = h1 + fdot(jnp.concatenate(mixed, axis=0), w_out)
    normed = (unit(h2) * gain2).astype(jnp.bfloat16)
    eps = 0.0
    for m in range(micro):
        rows = mix_rows(head_rows, m, micro, 16).astype(jnp.bfloat16)
        eps = eps + lax.dot_general(
            rows, normed[m * each : (m + 1) * each], NT, preferred_element_type=jnp.float32
        )
    return eps[: 3 * micro]


def alpha_bar(step):
    frac = (step / 1000.0 + 0.008) / 1.008
    return jnp.cos(frac * (math.pi / 2)) ** 2


def embed(step_ref, sec, chans):
    lane = lax.broadcasted_iota(jnp.int32, (16, chans), 1)
    row = lax.broadcasted_iota(jnp.int32, (16, chans), 0)
    half = chans // 2
    steps = jnp.zeros((16, chans), jnp.float32)
    for m in range(step_ref.shape[0]):
        steps = jnp.where(row == m, step_ref[m, sec].astype(jnp.float32), steps)
    angle = steps * jnp.exp(lax.rem(lane, half).astype(jnp.float32) * (-math.log(10000.0) / half))
    return jnp.where(lane < half, jnp.sin(angle), jnp.cos(angle)).astype(jnp.bfloat16)


def levels(step_ref, m, sec):
    step = jnp.full((8, 128), step_ref[m, sec].astype(jnp.float32))
    level, earlier = alpha_bar(step), alpha_bar(step - 50.0)
    out = (jnp.sqrt(1.0 - level), 1.0 / jnp.sqrt(level), jnp.sqrt(earlier), jnp.sqrt(1.0 - earlier))
    return [part[:1, :1] for part in out]


def denoise(noise, eps, step_ref, sec):
    micro = step_ref.shape[0]
    which = lax.rem(lax.broadcasted_iota(jnp.int32, eps.shape, 0), micro)
    table = [levels(step_ref, m, sec) for m in range(micro)]

    def scalar(n):
        out = jnp.broadcast_to(table[0][n], eps.shape)
        for m in range(1, micro):
            out = jnp.where(which == m, table[m][n], out)
        return out

    clean = jnp.clip((noise - scalar(0) * eps) * scalar(1), -1.0, 1.0)
    return clean, scalar(2) * clean + scalar(3) * eps


def begin(pairs, sems):
    copies = [pltpu.make_async_copy(src, dst, sems.at[n]) for n, (src, dst) in enumerate(pairs)]
    for copy in copies:
        copy.start()
    return copies


def front_kernel(step_ref, *refs):
    (
        text_hbm,
        t5_hbm,
        ids_hbm,
        base_x_hbm,
        first_x_hbm,
        base_in_hbm,
        base_gain_hbm,
        base_head_hbm,
        up_in_hbm,
        up_gain_hbm,
        up_head_hbm,
        up_time_hbm,
        up_conv_hbm,
        up_query_hbm,
        up_out_hbm,
        time_hbm,
        conv_hbm,
        query_hbm,
        out_hbm,
        kv_base_hbm,
        kv_up_hbm,
        noise_hbm,
    ) = refs[:22]
    kv_base_out, load_out, next_out, mine_out = refs[22:26]
    (
        text,
        t5_ref,
        ids_ref,
        base_x_ref,
        first_x_ref,
        base_in_ref,
        base_gain_ref,
        base_head_ref,
        up_in_ref,
        up_gain_ref,
        up_head_ref,
        up_time_ref,
        up_conv_ref,
        up_query_ref,
        up_out_ref,
        w_time,
        conv,
        w_query,
        w_out,
        kv_w,
        context,
        scales,
        kv_first,
        pad_base,
        taps,
        wide_x,
        pad_first,
        cols_first,
        sems,
    ) = refs[26:]
    seg, place = lax.axis_index("segment"), lax.axis_index("space")
    segments = lax.axis_size("segment")
    rows_text, dt5 = text.shape
    micro = base_x_ref.shape[1]
    ltxt = rows_text // micro
    cb, cs = base_gain_ref.shape[1], up_gain_ref.shape[2]
    px = base_x_ref.shape[2]
    side = math.isqrt(px)
    quarter = side // 4
    band = side // segments
    bf, f32 = jnp.bfloat16, jnp.float32
    step = kv_w.shape[2]
    half = step // 2
    n_base = kv_base_hbm.shape[1] // step
    chunks = [(kv_base_hbm.at[:, n * step : (n + 1) * step], kv_w.at[n]) for n in range(n_base)]
    chunks += [(kv_up_hbm.at[n], kv_w.at[n_base, :, n * half : (n + 1) * half]) for n in range(2)]
    early = (
        (base_x_hbm, base_x_ref),
        (base_in_hbm, base_in_ref),
        (base_gain_hbm, base_gain_ref),
        (time_hbm, w_time),
        (t5_hbm, t5_ref),
        (text_hbm, text),
    )
    small = (
        (ids_hbm, ids_ref),
        (first_x_hbm, first_x_ref),
        (base_head_hbm, base_head_ref),
        (up_in_hbm, up_in_ref),
        (up_gain_hbm, up_gain_ref),
        (up_head_hbm, up_head_ref),
        (up_time_hbm.at[0], up_time_ref),
        (up_conv_hbm.at[0], up_conv_ref),
        (up_query_hbm.at[0], up_query_ref),
        (up_out_hbm.at[0], up_out_ref),
    )
    ratio = mine_out.shape[1]
    late = ((conv_hbm, conv), (query_hbm, w_query), (out_hbm, w_out))
    late += ((noise_hbm.at[:, pl.ds(seg * ratio, ratio)], mine_out),)
    copies = begin(list(early) + list(small) + chunks[:n_base] + list(late[:3]) + chunks[n_base:] + list(late[3:]), sems)
    first_small = len(early)
    first_chunk = first_small + len(small)
    after = first_chunk + n_base

    for copy in copies[:4]:
        copy.wait()
    tall = quarter + 1
    temb = fdot(embed(step_ref, 0, cb), w_time[...])
    base_rows = [base_in_ref[c : c + 1].astype(f32) for c in range(3)]
    lanes = 128 * ((tall * side + 127) // 128)
    x_t = jnp.concatenate([plane_rows(base_x_ref, 0, lanes), jnp.zeros((2, lanes), f32)], axis=0)
    x_t = jnp.transpose(x_t)[: tall * side].astype(bf)
    pad_base[: 8 + side] = jnp.zeros((8 + side, cb), f32)
    edge = lax.broadcasted_iota(jnp.int32, (quarter, cb), 0) == 0
    corner_h = []
    for m in range(micro):
        h0 = fdot(x_t, mix_rows(base_rows, m, micro, 8).astype(bf)) + temb[m : m + 1]
        pad_base[8 + side : 8 + side + tall * side] = silu(unit(h0) * base_gain_ref[0:1])
        corner_h.append(
            jnp.concatenate([h0[side * h : side * h + quarter] for h in range(quarter)], axis=0)
        )
        for r in range(quarter + 1):
            for b in range(3):
                lo = pad_base[8 + side * r + b - 1 : 8 + side * r + b - 1 + quarter]
                hi = pad_base[8 + side * (r + 1) + b - 1 : 8 + side * (r + 1) + b - 1 + quarter]
                if b == 0:
                    lo, hi = jnp.where(edge, 0.0, lo), jnp.where(edge, 0.0, hi)
                both = jnp.concatenate([lo, hi], axis=0).astype(bf)
                for a in range(3):
                    h = r - a
                    if h % 2 == 0 and 0 <= h < quarter:
                        at = m * quarter * quarter + h * quarter
                        taps[at : at + 2 * quarter, (3 * a + b) * cb : (3 * a + b + 1) * cb] = both
    copies[4].wait()
    copies[5].wait()
    gain = t5_ref[...]

    lump = 512

    def prepare(i, carry):
        at = pl.multiple_of(i * 16, 16)
        sums = jnp.zeros((16, 128), f32)
        for c in range(0, dt5, lump):
            x = text[pl.ds(at, 16), c : c + lump].astype(f32)
            square = x * x
            for n in range(0, lump, 128):
                sums = sums + square[:, n : n + 128]
            context[pl.ds(at, 16), c : c + lump] = (x * gain[:, c : c + lump]).astype(bf)
        mean = jnp.sum(sums, axis=-1, keepdims=True) * (1.0 / dt5)
        scales[pl.ds(at, 16)] = jnp.broadcast_to(lax.rsqrt(mean + 1e-06), (16, 128))
        return carry

    lax.fori_loop(0, rows_text // 16, prepare, 0, unroll=2)
    for copy in copies[first_small:first_chunk]:
        copy.wait()
    biases = [key_bias(ids_ref, m, place) for m in range(micro)]
    scale = jnp.concatenate([scales[...]] * (step // 128), axis=1)
    for n in range(n_base):
        copies[first_chunk + n].wait()
        kv_base_out[:, n * step : (n + 1) * step] = (fdot(context[...], kv_w[n]) * scale).astype(bf)
    copies[after].wait()
    h1 = jnp.concatenate(corner_h, axis=0) + fdot(taps[...], conv[...])
    copies[after + 1].wait()
    copies[after + 2].wait()
    keyvals = [lambda at, m=m: kv_base_out[m * ltxt : (m + 1) * ltxt, at] for m in range(micro)]
    head_rows = [base_head_ref[c : c + 1].astype(f32) for c in range(3)]
    eps = back_part(
        h1, micro, keyvals, biases, base_gain_ref[1:2], base_gain_ref[2:3], w_query[...], w_out[...], head_rows
    )
    noise = plane_rows(base_x_ref, 0, lanes)
    noise = jnp.concatenate([noise[:, side * h : side * h + quarter] for h in range(quarter)], axis=1)
    corner, _ = denoise(noise, eps, step_ref, 0)

    for copy in copies[after + 3 :]:
        copy.wait()
    rest_kv = (fdot(context[...], kv_w[n_base]) * scale).astype(bf)
    kv_first[...] = rest_kv[:, :half]
    load_out[: micro * ltxt] = rest_kv[:, half:]
    near = 128 * ((2 * side + 127) // 128)
    window = near + band * side + near
    wide_x[...] = jnp.zeros_like(wide_x)
    wide_x[: 3 * micro, near : near + px] = plane_rows(first_x_ref, 0, px)
    x_win = wide_x[:, pl.ds(pl.multiple_of(seg * (band * side), 128), window)]
    spot = lax.broadcasted_iota(jnp.int32, (quarter * quarter, window), 0)
    pixel = lax.broadcasted_iota(jnp.int32, (quarter * quarter, window), 1) + (seg * band * side - near)
    rise = side // quarter
    hit = (lax.shift_right_arithmetic(pixel, (side * rise).bit_length() - 1) == lax.div(spot, quarter)) & (
        lax.div(lax.rem(pixel + 4 * px, side), rise) == lax.rem(spot, quarter)
    )
    corner16 = jnp.concatenate([corner, jnp.zeros((16 - 3 * micro, corner.shape[1]), f32)], axis=0).astype(bf)
    cond = fdot(corner16, jnp.where(hit, 1.0, 0.0).astype(bf))[:8]
    x_t = jnp.transpose(jnp.concatenate([x_win, cond], axis=0))
    skip = near - 2 * side
    total = (band + 4) * side
    x_t = x_t[skip : skip + total].astype(bf)
    temb = fdot(embed(step_ref, 1, cs), up_time_ref[...])
    up_rows = [up_in_ref[c, 0:1].astype(f32) for c in range(6)]
    kept = (band + 2) * side
    first_h, lhs = [], []
    for m in range(micro):
        rhs = jnp.concatenate(
            [mix_rows(up_rows[:3], m, micro, 8), mix_rows(up_rows[3:], m, micro, 8)], axis=0
        ).astype(bf)
        h0 = fdot(x_t, rhs) + temb[m : m + 1]
        act = inside_only(silu(unit(h0) * up_gain_ref[0, 0:1]), 2 * side, seg, segments)
        spread_cols(act, side, pad_first, cols_first.at[m])
        first_h.append(h0[side : side + kept])
        lhs.append(
            jnp.concatenate([cols_first[m, a * side : a * side + kept] for a in range(3)], axis=1)
        )
    h1 = jnp.concatenate(first_h, axis=0) + fdot(jnp.concatenate(lhs, axis=0), up_conv_ref[...].reshape(9 * cs, cs))
    keyvals = [lambda at, m=m: kv_first[m * ltxt : (m + 1) * ltxt, at] for m in range(micro)]
    head_rows = [up_head_ref[c, 0:1].astype(f32) for c in range(3)]
    eps = back_part(
        h1, micro, keyvals, biases, up_gain_ref[1, 0:1], up_gain_ref[2, 0:1], up_query_ref[...], up_out_ref[...],
        head_rows,
    )
    noise = x_win[: 3 * micro, near - side : near - side + kept]
    clean, prior = denoise(noise, eps, step_ref, 1)
    for c in range(3):
        next_out[c] = prior[c * micro : (c + 1) * micro, side : side + band * side].astype(bf)
    wide = load_out.shape[1]
    blocks = (load_out.shape[0] - micro * ltxt) // 16
    clean = jnp.concatenate([clean, jnp.zeros((3 * micro, blocks * wide - kept), f32)], axis=1)
    clean = jnp.concatenate([clean, jnp.zeros((16 - 3 * micro, blocks * wide), f32)], axis=0).astype(bf)
    for b in range(blocks):
        at = micro * ltxt + 16 * b
        load_out[at : at + 16] = clean[:, b * wide : (b + 1) * wide]


def base_kernel(step_ref, *refs):
    hbm, early_ref, vmem, extra = refs[:11], refs[11], refs[12:23], refs[23:]
    x_ref, w_in_ref, gain_ref, head_ref, time_ref, conv, ids_ref, next_ref, kv_ref, w_query, w_out = vmem
    wide_x, pad, cols, sems = extra
    seg, place = lax.axis_index("segment"), lax.axis_index("space")
    segments = lax.axis_size("segment")
    micro, px = x_ref.shape[1:]
    side = math.isqrt(px)
    band = side // segments
    ltxt = kv_ref.shape[0] // micro
    bf, f32 = jnp.bfloat16, jnp.float32
    copies = begin(list(zip(hbm, vmem)), sems)
    for copy in copies[:5]:
        copy.wait()
    chans = gain_ref.shape[1]
    near = 128 * ((side + 127) // 128)
    window = near + band * side + near
    wide_x[...] = jnp.zeros_like(wide_x)
    wide_x[: 3 * micro, near : near + px] = plane_rows(x_ref, 0, px)
    x_win = wide_x[:, pl.ds(pl.multiple_of(seg * (band * side), 128), window)]
    total = (band + 2) * side
    x_t = jnp.transpose(x_win)[near - side : near - side + total].astype(bf)
    temb = fdot(embed(step_ref, 0, chans), time_ref[...])
    rows = [w_in_ref[c : c + 1].astype(f32) for c in range(3)]
    kept = band * side
    hid, lhs = [], []
    for m in range(micro):
        h0 = fdot(x_t, mix_rows(rows, m, micro, 8).astype(bf)) + temb[m : m + 1]
        act = inside_only(silu(unit(h0) * gain_ref[0:1]), side, seg, segments)
        spread_cols(act, side, pad, cols.at[m])
        hid.append(h0[side : side + kept])
        lhs.append(jnp.concatenate([cols[m, a * side : a * side + kept] for a in range(3)], axis=1))
    copies[5].wait()
    h1 = jnp.concatenate(hid, axis=0) + fdot(jnp.concatenate(lhs, axis=0), conv[...])
    for copy in copies[6:]:
        copy.wait()
    biases = [key_bias(ids_ref, m, place) for m in range(micro)]
    keyvals = [lambda at, m=m: kv_ref[m * ltxt : (m + 1) * ltxt, at] for m in range(micro)]
    head_rows = [head_ref[c : c + 1].astype(f32) for c in range(3)]
    eps = back_part(
        h1, micro, keyvals, biases, gain_ref[1:2], gain_ref[2:3], w_query[...], w_out[...], head_rows
    )
    _, prior = denoise(x_win[: 3 * micro, near : near + kept], eps, step_ref, 0)
    for c in range(3):
        early_ref[0, c] = prior[c * micro : (c + 1) * micro].astype(bf)
    early_ref[1] = next_ref[...]


def like(array, index=None):
    shape = array.shape if index is None else array.shape[1:]
    return pltpu.VMEM(shape, array.dtype)


def front_call(segments, steps, ids, base_x, first_x, t5, base_w, up_w, text, kv_base_w, kv_up_w, noise, ratio):
    base_in, base_time, base_gain, base_conv, base_query, base_output, base_head = base_w
    up_in, up_time, up_gain, up_conv, up_query, up_out, up_head = up_w
    rows_text, dt5 = text.shape
    micro, px = base_x.shape[1:]
    side = math.isqrt(px)
    band = side // segments
    quarter = side // 4
    cb, cs = base_gain.shape[1], up_gain.shape[2]
    step = kv_up_w.shape[2]
    chunks = kv_base_w.shape[1] // step + 2
    near = 128 * ((2 * side + 127) // 128)
    blocks = -(-((band + 2) * side) // step)
    bf, f32 = jnp.bfloat16, jnp.float32
    smem = pl.BlockSpec(memory_space=pltpu.SMEM)
    vmem = pl.BlockSpec(memory_space=pltpu.VMEM)
    hbm = pl.BlockSpec(memory_space=pltpu.HBM)
    whole = (text, t5, ids, base_x, first_x, base_in, base_gain, base_head, up_in, up_gain, up_head)
    cut = (up_time, up_conv, up_query, up_out)
    big = (base_time, base_conv, base_query, base_output)
    args = whole + cut + big + (kv_base_w, kv_up_w, noise)
    return pl.pallas_call(
        front_kernel,
        out_shape=(
            jax.ShapeDtypeStruct((rows_text, 2 * cb), bf),
            jax.ShapeDtypeStruct((rows_text + 16 * blocks, step), bf),
            jax.ShapeDtypeStruct((3, micro, band * side), bf),
            jax.ShapeDtypeStruct(noise.shape[:1] + (ratio,) + noise.shape[2:], bf),
        ),
        in_specs=[smem] + [hbm] * len(args),
        out_specs=(vmem, vmem, vmem, vmem),
        scratch_shapes=[like(a) for a in whole]
        + [like(a, 0) for a in cut]
        + [like(a) for a in big]
        + [
            pltpu.VMEM((chunks // 2, dt5, 2 * step), bf),
            pltpu.VMEM((rows_text, dt5), bf),
            pltpu.VMEM((rows_text, 128), f32),
            pltpu.VMEM((rows_text, step), bf),
            pltpu.VMEM((16 + side + (quarter + 1) * side, cb), f32),
            pltpu.VMEM((micro * quarter * quarter, 9 * cb), bf),
            pltpu.VMEM((8, near + px + near), f32),
            pltpu.VMEM(((band + 4) * side + 16, cs), f32),
            pltpu.VMEM((micro, (band + 4) * side, 3 * cs), bf),
            pltpu.SemaphoreType.DMA((chunks + 20,)),
        ],
        compiler_params=pltpu.CompilerParams(vmem_limit_bytes=VMEM_ALL),
        cost_estimate=pl.CostEstimate(flops=5 * 10**9, bytes_accessed=22 * 10**6, transcendentals=10**6),
        name="text_and_first",
    )(steps, *args)


def base_call(segments, steps, ids, base_x, base_w, first_next, kv_base):
    base_in, base_time, base_gain, base_conv, base_query, base_output, base_head = base_w
    micro, px = base_x.shape[1:]
    side = math.isqrt(px)
    band = side // segments
    cb = base_gain.shape[1]
    near = 128 * ((side + 127) // 128)
    bf, f32 = jnp.bfloat16, jnp.float32
    smem = pl.BlockSpec(memory_space=pltpu.SMEM)
    vmem = pl.BlockSpec(memory_space=pltpu.VMEM)
    hbm = pl.BlockSpec(memory_space=pltpu.HBM)
    args = (base_x, base_in, base_gain, base_head, base_time, base_conv, ids, first_next, kv_base, base_query)
    args += (base_output,)
    return pl.pallas_call(
        base_kernel,
        out_shape=jax.ShapeDtypeStruct((2, 3, micro, band * side), bf),
        in_specs=[smem] + [hbm] * len(args),
        out_specs=vmem,
        scratch_shapes=[like(a) for a in args]
        + [
            pltpu.VMEM((8, near + px + near), f32),
            pltpu.VMEM(((band + 2) * side + 16, cb), f32),
            pltpu.VMEM((micro, (band + 2) * side, 3 * cb), bf),
            pltpu.SemaphoreType.DMA((len(args),)),
        ],
        compiler_params=pltpu.CompilerParams(vmem_limit_bytes=VMEM_ALL),
        cost_estimate=pl.CostEstimate(flops=4 * 10**9, bytes_accessed=7 * 10**6, transcendentals=10**6),
        name="base_section",
    )(steps, *args)


def last_kernel(ratio, tall, step_ref, *refs):
    hbm, out_ref = refs[: 11 + ratio], refs[11 + ratio]
    ids_ref, mine_ref, near_ref, far_ref, w_in_ref, gain_ref, head_ref, w_time_ref, conv_ref, query_ref, out_w_ref = refs[
        12 + ratio : 23 + ratio
    ]
    load, inbig, headbig, wpair, wq2, wo2, cond_pick, act, turn, *halves, sems = refs[23 + ratio :]
    slots = (halves[:3], halves[3:])
    seg, place = lax.axis_index("segment"), lax.axis_index("space")
    groups = lax.axis_size("space")
    micro = step_ref.shape[0]
    span = load.shape[1] - micro * LTXT
    pairs_io = [(hbm[4], w_in_ref), (hbm[5], gain_ref), (hbm[6], head_ref)]
    pairs_io += [(hbm[7 + n].at[1], ref) for n, ref in enumerate((w_time_ref, conv_ref, query_ref, out_w_ref))]
    pairs_io += [(hbm[0], ids_ref)]
    pairs_io += [(hbm[1 + n], ref) for n, ref in enumerate((mine_ref, near_ref, far_ref))]
    pairs_io += [(hbm[11 + k], load.at[k]) for k in range(ratio)]
    copies = begin(pairs_io, sems)
    chans = query_ref.shape[0]
    wide, high = mine_ref.shape[3:]
    ltxt = LTXT
    planes = 3 * wide
    phase = lax.rem(place, ratio)
    odd_place = lax.rem(place, 2) == 1
    cond_dev = high // tall
    pairs = wide // 2
    rows = high + 16
    lane2 = 2 * chans

    for copy in copies[:7]:
        copy.wait()
    bf = jnp.bfloat16
    sub = lax.broadcasted_iota(jnp.int32, (16, chans), 0)
    blank = jnp.zeros((16, chans), bf)
    spread_in = [jnp.broadcast_to(w_in_ref[c, 1:2].astype(jnp.float32), (16, chans)) for c in range(6)]
    spread_head = [jnp.broadcast_to(head_ref[c, 1:2].astype(jnp.float32), (16, chans)) for c in range(3)]
    for w in range(wide):
        lanes = slice(w * chans, (w + 1) * chans)
        here = sub == w % 16
        for rows_of, big in ((spread_in, inbig), (spread_head, headbig)):
            for c, row in enumerate(rows_of):
                one = jnp.where(here, row, 0.0).astype(bf)
                for n in range(wide // 16):
                    big[c * wide + 16 * n : c * wide + 16 * (n + 1), lanes] = one if n == w // 16 else blank
    zero_tap = jnp.zeros((chans, chans), jnp.bfloat16)
    for d in range(4):
        for a in range(3):
            at = (d * 3 + a) * chans
            wpair[at : at + chans, :chans] = conv_ref[3 * a + d] if d < 3 else zero_tap
            wpair[at : at + chans, chans:] = conv_ref[3 * a + d - 1] if d > 0 else zero_tap
    for dst, src in ((wq2, query_ref), (wo2, out_w_ref)):
        dst[:chans, :chans] = src[...]
        dst[:chans, chans:] = zero_tap
        dst[chans:, :chans] = zero_tap
        dst[chans:, chans:] = src[...]
    strip = cond_pick.shape[0] // 3
    pick_row = lax.broadcasted_iota(jnp.int32, (strip, planes), 0)
    pick_lane = lax.broadcasted_iota(jnp.int32, (strip, planes), 1)
    for c in range(3):
        hit = (pick_lane == c * wide + lax.rem(pick_row, wide))
        cond_pick[c * strip : (c + 1) * strip] = jnp.where(hit, 1.0, 0.0).astype(jnp.bfloat16)
    turn[...] = jnp.zeros_like(turn)
    for even, odd, _ in slots:
        even[0] = jnp.zeros(even.shape[1:], even.dtype)
        odd[pairs] = jnp.zeros(odd.shape[1:], odd.dtype)

    temb = fdot(embed(step_ref, 2, chans), w_time_ref[...])
    top_ok = jnp.where(place > 0, 1.0, 0.0)
    low_ok = jnp.where(place < groups - 1, 1.0, 0.0)
    gain0, gain1, gain2 = gain_ref[0, 1:2], gain_ref[1, 1:2], gain_ref[2, 1:2]
    inv = 1.0 / chans

    tile = lambda n: lax.div(lax.broadcasted_iota(jnp.int32, (lane2, lane2), n), chans)
    ones2 = jnp.where(tile(0) == tile(1), 1.0, 0.0).astype(jnp.bfloat16)
    gain0, gain1, gain2 = (jnp.concatenate([g, g], axis=1) for g in (gain0, gain1, gain2))

    def norm(x):
        total = fdot((x * x).astype(jnp.bfloat16), ones2)
        return x * lax.rsqrt(total * inv + 1e-06)

    tables = [levels(step_ref, m, 2) for m in range(micro)]
    for copy in copies[7:]:
        copy.wait()

    def lane_norm(x):
        return x * lax.rsqrt(jnp.sum(x * x, axis=-1, keepdims=True) * inv + 1e-06)

    duos = ratio // 2

    def spot(i):
        m, k = lax.div(i, ratio), lax.rem(i, ratio)
        duo = lax.rem(lax.div(phase, 2) - lax.rem(k, duos) + duos, duos)
        return m, k, 2 * duo + lax.rem(phase + lax.div(k, duos), 2)

    def front(i, slot):
        even, odd, hid = slots[slot]
        m, k, r = spot(i)
        temb_m = jnp.where(m == 0, temb[0:1], temb[1:2])
        temb2 = jnp.concatenate([temb_m, temb_m], axis=1)

        def window(ref, n):
            turn[n, :planes, :high] = ref[m, r].reshape(planes, high).astype(jnp.float32)
            return jnp.transpose(turn[n])

        body = window(mine_ref, 0)[:high, :planes]
        near = window(near_ref, 1)
        far = window(far_ref, 2)
        top = jnp.where(odd_place, near[high - 1 : high, :planes], far[high - 1 : high, :planes])
        low = jnp.where(odd_place, far[0:1, :planes], near[0:1, :planes])
        noise_rows = jnp.concatenate([body, top, low, jnp.zeros((14, planes), jnp.float32)], axis=0)
        blocks = [
            load[k, micro * ltxt + 16 * b : micro * ltxt + 16 * b + 8].astype(jnp.float32) for b in range(span // 16)
        ]
        band_planes = jnp.concatenate(blocks, axis=1)[:, :strip]
        row_h = lax.broadcasted_iota(jnp.int32, (rows, strip), 0)
        lane_px = lax.broadcasted_iota(jnp.int32, (rows, strip), 1)
        need = jnp.where(row_h < high, 1 + lax.div(row_h, tall), jnp.where(row_h == high, 0, cond_dev + 1))
        hit = lax.div(lane_px, wide) == need + phase * cond_dev
        spread = []
        for c in range(3):
            plane = jnp.where(m == 0, band_planes[2 * c : 2 * c + 1], band_planes[2 * c + 1 : 2 * c + 2])
            spread.append(jnp.where(hit, jnp.broadcast_to(plane, (rows, strip)), 0.0).astype(jnp.bfloat16))
        cond_rows = fdot(jnp.concatenate(spread, axis=1), cond_pick[...])
        pixels = jnp.concatenate([noise_rows, cond_rows], axis=1).astype(jnp.bfloat16)
        yield

        for t in range(pairs):
            h0 = fdot(pixels, inbig[:, t * lane2 : (t + 1) * lane2]) + temb2
            hid[t] = h0[:high]
            for par in range(2):
                x = silu(lane_norm(h0[:, par * chans : (par + 1) * chans]) * gain0[:, :chans])
                at = (t % 4) * 2 + par
                act[at, 8 : 8 + high] = x[:high]
                act[at, 7:8] = x[high : high + 1] * top_ok
                act[at, 8 + high : 9 + high] = x[high + 1 : high + 2] * low_ok
                wide3 = jnp.concatenate(
                    [act[at, 7 + a : 7 + a + high].astype(jnp.bfloat16) for a in range(3)], axis=1
                )
                if par == 0:
                    odd[t] = wide3
                else:
                    even[t + 1] = wide3
            if t % 2:
                yield

    subs = 2
    each = pairs // subs
    m_rows = each * high

    def back(i, slot):
        even, odd, hid = slots[slot]
        m, k, r = spot(i)
        keys = load[k, pl.ds(pl.multiple_of(m * ltxt, ltxt), ltxt), :chans]
        vals = load[k, pl.ds(pl.multiple_of(m * ltxt, ltxt), ltxt), chans:]
        kmask, vaug = pair_keys(keys, vals)
        bias = key_bias(ids_ref, m, seg * ratio + r)
        h1, mx = [], []
        for n in range(subs):
            at = n * each
            parts = (even[at : at + each], odd[at : at + each], even[at + 1 : at + 1 + each], odd[at + 1 : at + 1 + each])
            lhs = jnp.concatenate([part.reshape(m_rows, 3 * chans) for part in parts], axis=1)
            h1.append(fdot(lhs, wpair[...]) + hid[at : at + each].reshape(m_rows, lane2))
            yield
        query = []
        for n in range(subs):
            qn = fdot((norm(h1[n]) * gain1).astype(jnp.bfloat16), wq2[...])
            query.append((qn * (HD**-0.5 * LOG2E)).astype(jnp.bfloat16))
        yield
        for n in range(subs):
            mixed = []
            for p in range(2):
                mixed.append(attend_pair(query[n][:, p * chans : (p + 1) * chans], kmask, vaug, bias))
                yield
            mx.append(jnp.concatenate(mixed, axis=1))
        eps = jnp.zeros((planes, high), jnp.float32)
        for n in range(subs):
            h2 = h1[n] + fdot(mx[n], wo2[...])
            rows2 = (norm(h2) * gain2).astype(jnp.bfloat16).reshape(each, high, lane2)
            rows2 = jnp.concatenate([rows2[u] for u in range(each)], axis=1)
            eps = eps + lax.dot_general(
                headbig[:, n * each * lane2 : (n + 1) * each * lane2], rows2, NT, preferred_element_type=jnp.float32
            )
            yield
        noise = mine_ref[m, r].reshape(planes, high).astype(jnp.float32)
        ca, cb, cc, cd = (jnp.where(m == 0, tables[0][n], tables[1][n]) for n in range(4))
        clean = jnp.clip((noise - ca * eps) * cb, -1.0, 1.0)
        prior = cc * clean + cd * eps
        out_ref[0, m, r] = clean.astype(jnp.bfloat16).reshape(3, wide, high)
        out_ref[1, m, r] = prior.astype(jnp.bfloat16).reshape(3, wide, high)

    def together(*streams):
        live = list(streams)
        while live:
            live = [stream for stream in live if next(stream, stop) is not stop]

    stop = object()
    total = micro * ratio

    def couple(j, carry):
        together(back(2 * j, 0), front(2 * j + 1, 1))
        together(back(2 * j + 1, 1), front(2 * j + 2, 0))
        return carry

    together(front(0, 0))
    lax.fori_loop(0, total // 2 - 1, couple, 0)
    together(back(total - 2, 0), front(total - 1, 1))
    together(back(total - 1, 1))


def last_call(ratio, tall, steps, ids, noise, near, far, loads, weights):
    w_in, w_time, gains, w_conv, w_query, w_out, head = weights
    micro, _, _, wide, high = noise.shape
    chans = w_query.shape[1]
    planes = 3 * wide
    pairs = wide // 2
    strip = 512
    smem = pl.BlockSpec(memory_space=pltpu.SMEM)
    vmem = pl.BlockSpec(memory_space=pltpu.VMEM)
    hbm = pl.BlockSpec(memory_space=pltpu.HBM)
    bf, f32 = jnp.bfloat16, jnp.float32
    args = (ids, noise, near, far, w_in, gains, head, w_time, w_conv, w_query, w_out) + tuple(loads)
    part = pltpu.VMEM((micro, ratio, 3, wide, high), bf)
    return pl.pallas_call(
        functools.partial(last_kernel, ratio, tall),
        out_shape=jax.ShapeDtypeStruct((2, micro, ratio, 3, wide, high), bf),
        in_specs=[smem] + [hbm] * len(args),
        out_specs=vmem,
        scratch_shapes=[like(ids), part, part, part, like(w_in), like(gains), like(head)]
        + [like(a, 0) for a in (w_time, w_conv, w_query, w_out)]
        + [
            pltpu.VMEM((ratio,) + loads[0].shape, bf),
            pltpu.VMEM((2 * planes, wide * chans), bf),
            pltpu.VMEM((planes, wide * chans), bf),
            pltpu.VMEM((12 * chans, 2 * chans), bf),
            pltpu.VMEM((2 * chans, 2 * chans), bf),
            pltpu.VMEM((2 * chans, 2 * chans), bf),
            pltpu.VMEM((3 * strip, planes), bf),
            pltpu.VMEM((8, high + 16, chans), f32),
            pltpu.VMEM((3, 128, 128), f32),
        ]
        + [
            pltpu.VMEM((pairs + 1, high, 3 * chans), bf),
            pltpu.VMEM((pairs + 1, high, 3 * chans), bf),
            pltpu.VMEM((pairs, high, 2 * chans), f32),
        ]
        * 2
        + [
            pltpu.SemaphoreType.DMA((len(args),)),
        ],
        compiler_params=pltpu.CompilerParams(vmem_limit_bytes=VMEM_ALL),
        cost_estimate=pl.CostEstimate(flops=10**10, bytes_accessed=4 * 10**6, transcendentals=10**7),
        name="last_section",
    )(steps, *args)


def shards(
    text_states,
    token_ids,
    step_ids,
    base_noise,
    upscale_noise,
    final_noise,
    t5_gain,
    base_keyval,
    upscale_keyval,
    base_input,
    base_time,
    base_gain,
    base_conv,
    base_query,
    base_output,
    base_head,
    upscale_input,
    upscale_time,
    upscale_gain,
    upscale_conv,
    upscale_query,
    upscale_output,
    upscale_head,
):
    groups = lax.axis_size("space")
    segments = lax.axis_size("segment")
    ratio = groups // segments
    micro, _, ltxt, dt5 = text_states.shape
    rows_dev, cols = final_noise.shape[3:]
    tall = rows_dev * groups // cols

    noise_t = final_noise.swapaxes(3, 4)
    steps = step_ids.T
    chans_base = base_query.shape[1]
    base_x = base_noise.transpose(1, 2, 0, 3)[0]
    first_x = upscale_noise.transpose(1, 2, 0, 3)[0]
    base_w = (
        base_input,
        base_time,
        base_gain,
        base_conv.reshape(9 * chans_base, chans_base),
        base_query,
        base_output,
        base_head.T,
    )
    up_in = upscale_input.transpose(1, 0, 2)
    up_gain = upscale_gain.transpose(1, 0, 2)
    up_head = upscale_head.transpose(2, 0, 1)
    up_w = (up_in, upscale_time, up_gain, upscale_conv, upscale_query, upscale_output, up_head)
    kv_base, bundle, first_next, mine = front_call(
        segments,
        steps,
        token_ids,
        base_x,
        first_x,
        t5_gain[None],
        base_w,
        up_w,
        text_states.reshape(micro * ltxt, dt5),
        base_keyval,
        upscale_keyval,
        noise_t,
        ratio,
    )
    duos = ratio // 2
    cross = [
        [
            (s * groups + ratio * q + r, q * groups + ratio * s + 2 * ((r // 2 + k) % duos) + r % 2)
            for s in range(segments)
            for q in range(segments)
            for r in range(ratio)
        ]
        for k in range(duos)
    ]
    got = [lax.ppermute(bundle, ("segment", "space"), cross[k]) for k in range(duos)]
    swaps = [(i, i + 1) for i in range(0, groups - 1, 2)]
    near = lax.ppermute(mine, "space", swaps + [(j, i) for i, j in swaps])
    swaps = [(i, i + 1) for i in range(1, groups - 1, 2)]
    far = lax.ppermute(mine, "space", swaps + [(j, i) for i, j in swaps])

    early = base_call(segments, steps, token_ids, base_x, base_w, first_next, kv_base)
    mates = [(i, i ^ 1) for i in range(groups)]
    got, early = lax.optimization_barrier((got, early))
    loads = got + [lax.ppermute(array, "space", mates) for array in got]
    final = last_call(ratio, tall, steps, token_ids, mine, near, far, loads, up_w)
    early_states = early.transpose(0, 2, 1, 3)[:, :, None]
    return early_states, final.swapaxes(4, 5)


def solution(mesh):
    placed = (
        P(None, "space", None, None),
        P(),
        P(),
        P(None, "space", None, None),
        P(None, "space", None, None),
        P(None, None, None, "space", None),
    ) + (P(),) * 17

    return jax.shard_map(
        shards,
        mesh=mesh,
        in_specs=placed,
        out_specs=(
            P(None, None, "space", None, "segment"),
            P(None, None, "segment", None, "space", None),
        ),
        check_vma=False,
    )
```

```python
import functools
import math

import jax
import jax.numpy as jnp
from jax import lax
from jax.experimental import pallas as pl
from jax.experimental.pallas import tpu as pltpu
from jax.sharding import PartitionSpec as P


HD = 64
LTXT = 128
VMEM_ALL = 67043328
LOG2E = math.log2(math.e)


NT = (((1,), (1,)), ((), ()))


def unit(x):
    return x * lax.rsqrt(jnp.sum(x * x, axis=-1, keepdims=True) * (1.0 / x.shape[-1]) + 1e-06)


def silu(x):
    return x * (0.5 + 0.5 * jnp.tanh(0.5 * x))


def fdot(a, b):
    return jnp.dot(a, b, preferred_element_type=jnp.float32)


def plane_rows(ref, at, size):
    parts = [ref[c, :, pl.ds(at, size)].astype(jnp.float32) for c in range(ref.shape[0])]
    return jnp.concatenate(parts, axis=0)


def mix_rows(rows, m, micro, total):
    zero = jnp.zeros_like(rows[0])
    out = [row if n == m else zero for row in rows for n in range(micro)]
    if total > len(out):
        out.append(jnp.zeros((total - len(out), rows[0].shape[1]), rows[0].dtype))
    return jnp.concatenate(out, axis=0)


def spread_cols(act, side, pad, dst):
    count, chans = act.shape
    pad[8 : 8 + count] = act
    col = lax.broadcasted_iota(jnp.int32, (1, side, chans), 1)
    left = pad[7 : 7 + count].reshape(count // side, side, chans)
    right = pad[9 : 9 + count].reshape(count // side, side, chans)
    left = jnp.where(col == 0, 0.0, left).reshape(count, chans)
    right = jnp.where(col == side - 1, 0.0, right).reshape(count, chans)
    dst[:, :chans] = left.astype(jnp.bfloat16)
    dst[:, chans : 2 * chans] = act.astype(jnp.bfloat16)
    dst[:, 2 * chans :] = right.astype(jnp.bfloat16)


def inside_only(act, outer, seg, segments):
    top = act[:outer] * jnp.where(seg > 0, 1.0, 0.0)
    low = act[act.shape[0] - outer :] * jnp.where(seg < segments - 1, 1.0, 0.0)
    return jnp.concatenate([top, act[outer : act.shape[0] - outer], low], axis=0)


def pair_keys(keys, vals):
    first = lax.broadcasted_iota(jnp.int32, keys.shape, 1) < HD
    keys, vals = keys.astype(jnp.float32), vals.astype(jnp.float32)
    kmask = jnp.concatenate([jnp.where(first, keys, 0.0), jnp.where(first, 0.0, keys)], axis=0)
    upper = jnp.concatenate([jnp.where(first, vals, 0.0), jnp.where(first, 1.0, 0.0)], axis=1)
    lower = jnp.concatenate([jnp.where(first, 0.0, vals), jnp.where(first, 0.0, 1.0)], axis=1)
    return kmask.astype(jnp.bfloat16), jnp.concatenate([upper, lower], axis=0).astype(jnp.bfloat16)


def attend_pair(query, kmask, vaug, bias):
    lanes = query.shape[1]
    half = kmask.shape[0] // 2
    scores = lax.dot_general(query, kmask, NT, preferred_element_type=jnp.float32) + bias
    probs = []
    for e in range(2):
        part = scores[:, e * half : (e + 1) * half]
        probs.append(jnp.exp2(part - jnp.max(part, axis=-1, keepdims=True)).astype(jnp.bfloat16))
    both = fdot(jnp.concatenate(probs, axis=1), vaug)
    return (both[:, :lanes] / both[:, lanes:]).astype(jnp.bfloat16)


def key_bias(ids_ref, m, who):
    bias = jnp.where(ids_ref[m, pl.ds(who, 1)] == 0, -1e30, 0.0)
    return jnp.concatenate([bias, bias], axis=1)


def back_part(h1, micro, keyvals, biases, gain1, gain2, w_query, w_out, head_rows):
    count, width = h1.shape
    each = count // micro
    query = fdot((unit(h1) * gain1).astype(jnp.bfloat16), w_query)
    query = (query * (HD**-0.5 * LOG2E)).astype(jnp.bfloat16)
    mixed = []
    for m in range(micro):
        cols = []
        for g in range(width // (2 * HD)):
            at = slice(2 * HD * g, 2 * HD * (g + 1))
            kmask, vaug = pair_keys(keyvals[m](at), keyvals[m](slice(width + at.start, width + at.stop)))
            cols.append(attend_pair(query[m * each : (m + 1) * each, at], kmask, vaug, biases[m]))
        mixed.append(jnp.concatenate(cols, axis=1) if len(cols) > 1 else cols[0])
    h2 = h1 + fdot(jnp.concatenate(mixed, axis=0), w_out)
    normed = (unit(h2) * gain2).astype(jnp.bfloat16)
    eps = 0.0
    for m in range(micro):
        rows = mix_rows(head_rows, m, micro, 16).astype(jnp.bfloat16)
        eps = eps + lax.dot_general(
            rows, normed[m * each : (m + 1) * each], NT, preferred_element_type=jnp.float32
        )
    return eps[: 3 * micro]


def alpha_bar(step):
    frac = (step / 1000.0 + 0.008) / 1.008
    return jnp.cos(frac * (math.pi / 2)) ** 2


def embed(step_ref, sec, chans):
    lane = lax.broadcasted_iota(jnp.int32, (16, chans), 1)
    row = lax.broadcasted_iota(jnp.int32, (16, chans), 0)
    half = chans // 2
    steps = jnp.zeros((16, chans), jnp.float32)
    for m in range(step_ref.shape[0]):
        steps = jnp.where(row == m, step_ref[m, sec].astype(jnp.float32), steps)
    angle = steps * jnp.exp(lax.rem(lane, half).astype(jnp.float32) * (-math.log(10000.0) / half))
    return jnp.where(lane < half, jnp.sin(angle), jnp.cos(angle)).astype(jnp.bfloat16)


def levels(step_ref, m, sec):
    step = jnp.full((8, 128), step_ref[m, sec].astype(jnp.float32))
    level, earlier = alpha_bar(step), alpha_bar(step - 50.0)
    out = (jnp.sqrt(1.0 - level), 1.0 / jnp.sqrt(level), jnp.sqrt(earlier), jnp.sqrt(1.0 - earlier))
    return [part[:1, :1] for part in out]


def denoise(noise, eps, step_ref, sec):
    micro = step_ref.shape[0]
    which = lax.rem(lax.broadcasted_iota(jnp.int32, eps.shape, 0), micro)
    table = [levels(step_ref, m, sec) for m in range(micro)]

    def scalar(n):
        out = jnp.broadcast_to(table[0][n], eps.shape)
        for m in range(1, micro):
            out = jnp.where(which == m, table[m][n], out)
        return out

    clean = jnp.clip((noise - scalar(0) * eps) * scalar(1), -1.0, 1.0)
    return clean, scalar(2) * clean + scalar(3) * eps


def begin(pairs, sems):
    copies = [pltpu.make_async_copy(src, dst, sems.at[n]) for n, (src, dst) in enumerate(pairs)]
    for copy in copies:
        copy.start()
    return copies


def front_kernel(step_ref, *refs):
    (
        text_hbm,
        t5_hbm,
        ids_hbm,
        base_x_hbm,
        first_x_hbm,
        base_in_hbm,
        base_gain_hbm,
        base_head_hbm,
        up_in_hbm,
        up_gain_hbm,
        up_head_hbm,
        up_time_hbm,
        up_conv_hbm,
        up_query_hbm,
        up_out_hbm,
        time_hbm,
        conv_hbm,
        query_hbm,
        out_hbm,
        kv_base_hbm,
        kv_up_hbm,
        noise_hbm,
    ) = refs[:22]
    kv_base_out, load_out, next_out, mine_out = refs[22:26]
    (
        text,
        t5_ref,
        ids_ref,
        base_x_ref,
        first_x_ref,
        base_in_ref,
        base_gain_ref,
        base_head_ref,
        up_in_ref,
        up_gain_ref,
        up_head_ref,
        up_time_ref,
        up_conv_ref,
        up_query_ref,
        up_out_ref,
        w_time,
        conv,
        w_query,
        w_out,
        kv_w,
        context,
        scales,
        kv_first,
        pad_base,
        taps,
        wide_x,
        pad_first,
        cols_first,
        sems,
    ) = refs[26:]
    seg, place = lax.axis_index("segment"), lax.axis_index("space")
    segments = lax.axis_size("segment")
    rows_text, dt5 = text.shape
    micro = base_x_ref.shape[1]
    ltxt = rows_text // micro
    cb, cs = base_gain_ref.shape[1], up_gain_ref.shape[2]
    px = base_x_ref.shape[2]
    side = math.isqrt(px)
    quarter = side // 4
    band = side // segments
    bf, f32 = jnp.bfloat16, jnp.float32
    step = kv_w.shape[2]
    half = step // 2
    n_base = kv_base_hbm.shape[1] // step
    chunks = [(kv_base_hbm.at[:, n * step : (n + 1) * step], kv_w.at[n]) for n in range(n_base)]
    chunks += [(kv_up_hbm.at[n], kv_w.at[n_base, :, n * half : (n + 1) * half]) for n in range(2)]
    early = (
        (base_x_hbm, base_x_ref),
        (base_in_hbm, base_in_ref),
        (base_gain_hbm, base_gain_ref),
        (time_hbm, w_time),
        (t5_hbm, t5_ref),
        (text_hbm, text),
    )
    small = (
        (ids_hbm, ids_ref),
        (first_x_hbm, first_x_ref),
        (base_head_hbm, base_head_ref),
        (up_in_hbm, up_in_ref),
        (up_gain_hbm, up_gain_ref),
        (up_head_hbm, up_head_ref),
        (up_time_hbm.at[0], up_time_ref),
        (up_conv_hbm.at[0], up_conv_ref),
        (up_query_hbm.at[0], up_query_ref),
        (up_out_hbm.at[0], up_out_ref),
    )
    ratio = mine_out.shape[1]
    third = 3 * cb
    late = tuple((conv_hbm.at[a * third : (a + 1) * third], conv.at[a * third : (a + 1) * third]) for a in range(3))
    late += ((query_hbm, w_query), (out_hbm, w_out))
    late += ((noise_hbm.at[:, pl.ds(seg * ratio, ratio)], mine_out),)
    copies = begin(list(early) + list(small) + chunks[:n_base] + list(late[:5]) + chunks[n_base:] + list(late[5:]), sems)
    first_small = len(early)
    first_chunk = first_small + len(small)
    after = first_chunk + n_base

    for copy in copies[:4]:
        copy.wait()
    tall = quarter + 1
    temb = fdot(embed(step_ref, 0, cb), w_time[...])
    base_rows = [base_in_ref[c : c + 1].astype(f32) for c in range(3)]
    lanes = 128 * ((tall * side + 127) // 128)
    x_t = jnp.concatenate([plane_rows(base_x_ref, 0, lanes), jnp.zeros((2, lanes), f32)], axis=0)
    x_t = jnp.transpose(x_t)[: tall * side].astype(bf)
    pad_base[: 8 + side] = jnp.zeros((8 + side, cb), f32)
    edge = lax.broadcasted_iota(jnp.int32, (quarter, cb), 0) == 0
    corner_h = []
    for m in range(micro):
        h0 = fdot(x_t, mix_rows(base_rows, m, micro, 8).astype(bf)) + temb[m : m + 1]
        pad_base[8 + side : 8 + side + tall * side] = silu(unit(h0) * base_gain_ref[0:1])
        corner_h.append(
            jnp.concatenate([h0[side * h : side * h + quarter] for h in range(quarter)], axis=0)
        )
        for r in range(quarter + 1):
            for b in range(3):
                lo = pad_base[8 + side * r + b - 1 : 8 + side * r + b - 1 + quarter]
                hi = pad_base[8 + side * (r + 1) + b - 1 : 8 + side * (r + 1) + b - 1 + quarter]
                if b == 0:
                    lo, hi = jnp.where(edge, 0.0, lo), jnp.where(edge, 0.0, hi)
                both = jnp.concatenate([lo, hi], axis=0).astype(bf)
                for a in range(3):
                    h = r - a
                    if h % 2 == 0 and 0 <= h < quarter:
                        at = m * quarter * quarter + h * quarter
                        taps[at : at + 2 * quarter, (3 * a + b) * cb : (3 * a + b + 1) * cb] = both
    copies[4].wait()
    copies[5].wait()
    gain = t5_ref[...]

    lump = 512

    def prepare(i, carry):
        at = pl.multiple_of(i * 16, 16)
        sums = jnp.zeros((16, 128), f32)
        for c in range(0, dt5, lump):
            x = text[pl.ds(at, 16), c : c + lump].astype(f32)
            square = x * x
            for n in range(0, lump, 128):
                sums = sums + square[:, n : n + 128]
            context[pl.ds(at, 16), c : c + lump] = (x * gain[:, c : c + lump]).astype(bf)
        mean = jnp.sum(sums, axis=-1, keepdims=True) * (1.0 / dt5)
        scales[pl.ds(at, 16)] = jnp.broadcast_to(lax.rsqrt(mean + 1e-06), (16, 128))
        return carry

    lax.fori_loop(0, rows_text // 16, prepare, 0, unroll=2)
    for copy in copies[first_small:first_chunk]:
        copy.wait()
    biases = [key_bias(ids_ref, m, place) for m in range(micro)]
    scale = jnp.concatenate([scales[...]] * (step // 128), axis=1)
    for n in range(n_base):
        copies[first_chunk + n].wait()
        kv_base_out[:, n * step : (n + 1) * step] = (fdot(context[...], kv_w[n]) * scale).astype(bf)
    h1 = jnp.concatenate(corner_h, axis=0)
    for a in range(3):
        copies[after + a].wait()
        h1 = h1 + fdot(taps[:, a * third : (a + 1) * third], conv[a * third : (a + 1) * third])
    copies[after + 3].wait()
    copies[after + 4].wait()
    keyvals = [lambda at, m=m: kv_base_out[m * ltxt : (m + 1) * ltxt, at] for m in range(micro)]
    head_rows = [base_head_ref[c : c + 1].astype(f32) for c in range(3)]
    eps = back_part(
        h1, micro, keyvals, biases, base_gain_ref[1:2], base_gain_ref[2:3], w_query[...], w_out[...], head_rows
    )
    noise = plane_rows(base_x_ref, 0, lanes)
    noise = jnp.concatenate([noise[:, side * h : side * h + quarter] for h in range(quarter)], axis=1)
    corner, _ = denoise(noise, eps, step_ref, 0)

    for copy in copies[after + 5 :]:
        copy.wait()
    rest_kv = (fdot(context[...], kv_w[n_base]) * scale).astype(bf)
    kv_first[...] = rest_kv[:, :half]
    load_out[: micro * ltxt] = rest_kv[:, half:]
    near = 128 * ((2 * side + 127) // 128)
    window = near + band * side + near
    wide_x[...] = jnp.zeros_like(wide_x)
    wide_x[: 3 * micro, near : near + px] = plane_rows(first_x_ref, 0, px)
    x_win = wide_x[:, pl.ds(pl.multiple_of(seg * (band * side), 128), window)]
    spot = lax.broadcasted_iota(jnp.int32, (quarter * quarter, window), 0)
    pixel = lax.broadcasted_iota(jnp.int32, (quarter * quarter, window), 1) + (seg * band * side - near)
    rise = side // quarter
    hit = (lax.shift_right_arithmetic(pixel, (side * rise).bit_length() - 1) == lax.div(spot, quarter)) & (
        lax.div(lax.rem(pixel + 4 * px, side), rise) == lax.rem(spot, quarter)
    )
    corner16 = jnp.concatenate([corner, jnp.zeros((16 - 3 * micro, corner.shape[1]), f32)], axis=0).astype(bf)
    cond = fdot(corner16, jnp.where(hit, 1.0, 0.0).astype(bf))[:8]
    x_t = jnp.transpose(jnp.concatenate([x_win, cond], axis=0))
    skip = near - 2 * side
    total = (band + 4) * side
    x_t = x_t[skip : skip + total].astype(bf)
    temb = fdot(embed(step_ref, 1, cs), up_time_ref[...])
    up_rows = [up_in_ref[c, 0:1].astype(f32) for c in range(6)]
    kept = (band + 2) * side
    first_h, lhs = [], []
    for m in range(micro):
        rhs = jnp.concatenate(
            [mix_rows(up_rows[:3], m, micro, 8), mix_rows(up_rows[3:], m, micro, 8)], axis=0
        ).astype(bf)
        h0 = fdot(x_t, rhs) + temb[m : m + 1]
        act = inside_only(silu(unit(h0) * up_gain_ref[0, 0:1]), 2 * side, seg, segments)
        spread_cols(act, side, pad_first, cols_first.at[m])
        first_h.append(h0[side : side + kept])
        lhs.append(
            jnp.concatenate([cols_first[m, a * side : a * side + kept] for a in range(3)], axis=1)
        )
    h1 = jnp.concatenate(first_h, axis=0) + fdot(jnp.concatenate(lhs, axis=0), up_conv_ref[...].reshape(9 * cs, cs))
    keyvals = [lambda at, m=m: kv_first[m * ltxt : (m + 1) * ltxt, at] for m in range(micro)]
    head_rows = [up_head_ref[c, 0:1].astype(f32) for c in range(3)]
    eps = back_part(
        h1, micro, keyvals, biases, up_gain_ref[1, 0:1], up_gain_ref[2, 0:1], up_query_ref[...], up_out_ref[...],
        head_rows,
    )
    noise = x_win[: 3 * micro, near - side : near - side + kept]
    clean, prior = denoise(noise, eps, step_ref, 1)
    for c in range(3):
        next_out[c] = prior[c * micro : (c + 1) * micro, side : side + band * side].astype(bf)
    wide = load_out.shape[1]
    blocks = (load_out.shape[0] - micro * ltxt) // 16
    clean = jnp.concatenate([clean, jnp.zeros((3 * micro, blocks * wide - kept), f32)], axis=1)
    clean = jnp.concatenate([clean, jnp.zeros((16 - 3 * micro, blocks * wide), f32)], axis=0).astype(bf)
    for b in range(blocks):
        at = micro * ltxt + 16 * b
        load_out[at : at + 16] = clean[:, b * wide : (b + 1) * wide]


def base_kernel(step_ref, *refs):
    hbm, early_ref, vmem, extra = refs[:11], refs[11], refs[12:23], refs[23:]
    x_ref, w_in_ref, gain_ref, head_ref, time_ref, conv, ids_ref, next_ref, kv_ref, w_query, w_out = vmem
    wide_x, pad, cols, sems = extra
    seg, place = lax.axis_index("segment"), lax.axis_index("space")
    segments = lax.axis_size("segment")
    micro, px = x_ref.shape[1:]
    side = math.isqrt(px)
    band = side // segments
    ltxt = kv_ref.shape[0] // micro
    bf, f32 = jnp.bfloat16, jnp.float32
    plan = list(zip(hbm, vmem))
    third = conv.shape[0] // 3
    cuts = [tuple(ref.at[a * third : (a + 1) * third] for ref in plan[5]) for a in range(3)]
    copies = begin(plan[:5] + cuts + plan[6:], sems)
    for copy in copies[:5]:
        copy.wait()
    chans = gain_ref.shape[1]
    near = 128 * ((side + 127) // 128)
    window = near + band * side + near
    wide_x[...] = jnp.zeros_like(wide_x)
    wide_x[: 3 * micro, near : near + px] = plane_rows(x_ref, 0, px)
    x_win = wide_x[:, pl.ds(pl.multiple_of(seg * (band * side), 128), window)]
    total = (band + 2) * side
    x_t = jnp.transpose(x_win)[near - side : near - side + total].astype(bf)
    temb = fdot(embed(step_ref, 0, chans), time_ref[...])
    rows = [w_in_ref[c : c + 1].astype(f32) for c in range(3)]
    kept = band * side
    hid = []
    for m in range(micro):
        h0 = fdot(x_t, mix_rows(rows, m, micro, 8).astype(bf)) + temb[m : m + 1]
        act = inside_only(silu(unit(h0) * gain_ref[0:1]), side, seg, segments)
        spread_cols(act, side, pad, cols.at[m])
        hid.append(h0[side : side + kept])
    h1 = jnp.concatenate(hid, axis=0)
    for a in range(3):
        copies[5 + a].wait()
        lhs = jnp.concatenate([cols[m, a * side : a * side + kept] for m in range(micro)], axis=0)
        h1 = h1 + fdot(lhs, conv[a * third : (a + 1) * third])
    for copy in copies[8:]:
        copy.wait()
    biases = [key_bias(ids_ref, m, place) for m in range(micro)]
    keyvals = [lambda at, m=m: kv_ref[m * ltxt : (m + 1) * ltxt, at] for m in range(micro)]
    head_rows = [head_ref[c : c + 1].astype(f32) for c in range(3)]
    eps = back_part(
        h1, micro, keyvals, biases, gain_ref[1:2], gain_ref[2:3], w_query[...], w_out[...], head_rows
    )
    _, prior = denoise(x_win[: 3 * micro, near : near + kept], eps, step_ref, 0)
    for c in range(3):
        early_ref[0, c] = prior[c * micro : (c + 1) * micro].astype(bf)
    early_ref[1] = next_ref[...]


def like(array, index=None):
    shape = array.shape if index is None else array.shape[1:]
    return pltpu.VMEM(shape, array.dtype)


def front_call(segments, steps, ids, base_x, first_x, t5, base_w, up_w, text, kv_base_w, kv_up_w, noise, ratio):
    base_in, base_time, base_gain, base_conv, base_query, base_output, base_head = base_w
    up_in, up_time, up_gain, up_conv, up_query, up_out, up_head = up_w
    rows_text, dt5 = text.shape
    micro, px = base_x.shape[1:]
    side = math.isqrt(px)
    band = side // segments
    quarter = side // 4
    cb, cs = base_gain.shape[1], up_gain.shape[2]
    step = kv_up_w.shape[2]
    chunks = kv_base_w.shape[1] // step + 2
    near = 128 * ((2 * side + 127) // 128)
    blocks = -(-((band + 2) * side) // step)
    bf, f32 = jnp.bfloat16, jnp.float32
    smem = pl.BlockSpec(memory_space=pltpu.SMEM)
    vmem = pl.BlockSpec(memory_space=pltpu.VMEM)
    hbm = pl.BlockSpec(memory_space=pltpu.HBM)
    whole = (text, t5, ids, base_x, first_x, base_in, base_gain, base_head, up_in, up_gain, up_head)
    cut = (up_time, up_conv, up_query, up_out)
    big = (base_time, base_conv, base_query, base_output)
    args = whole + cut + big + (kv_base_w, kv_up_w, noise)
    return pl.pallas_call(
        front_kernel,
        out_shape=(
            jax.ShapeDtypeStruct((rows_text, 2 * cb), bf),
            jax.ShapeDtypeStruct((rows_text + 16 * blocks, step), bf),
            jax.ShapeDtypeStruct((3, micro, band * side), bf),
            jax.ShapeDtypeStruct(noise.shape[:1] + (ratio,) + noise.shape[2:], bf),
        ),
        in_specs=[smem] + [hbm] * len(args),
        out_specs=(vmem, vmem, vmem, vmem),
        scratch_shapes=[like(a) for a in whole]
        + [like(a, 0) for a in cut]
        + [like(a) for a in big]
        + [
            pltpu.VMEM((chunks // 2, dt5, 2 * step), bf),
            pltpu.VMEM((rows_text, dt5), bf),
            pltpu.VMEM((rows_text, 128), f32),
            pltpu.VMEM((rows_text, step), bf),
            pltpu.VMEM((16 + side + (quarter + 1) * side, cb), f32),
            pltpu.VMEM((micro * quarter * quarter, 9 * cb), bf),
            pltpu.VMEM((8, near + px + near), f32),
            pltpu.VMEM(((band + 4) * side + 16, cs), f32),
            pltpu.VMEM((micro, (band + 4) * side, 3 * cs), bf),
            pltpu.SemaphoreType.DMA((chunks + 22,)),
        ],
        compiler_params=pltpu.CompilerParams(vmem_limit_bytes=VMEM_ALL),
        cost_estimate=pl.CostEstimate(flops=5 * 10**9, bytes_accessed=22 * 10**6, transcendentals=10**6),
        name="text_and_first",
    )(steps, *args)


def base_call(segments, steps, ids, base_x, base_w, first_next, kv_base):
    base_in, base_time, base_gain, base_conv, base_query, base_output, base_head = base_w
    micro, px = base_x.shape[1:]
    side = math.isqrt(px)
    band = side // segments
    cb = base_gain.shape[1]
    near = 128 * ((side + 127) // 128)
    bf, f32 = jnp.bfloat16, jnp.float32
    smem = pl.BlockSpec(memory_space=pltpu.SMEM)
    vmem = pl.BlockSpec(memory_space=pltpu.VMEM)
    hbm = pl.BlockSpec(memory_space=pltpu.HBM)
    args = (base_x, base_in, base_gain, base_head, base_time, base_conv, ids, first_next, kv_base, base_query)
    args += (base_output,)
    return pl.pallas_call(
        base_kernel,
        out_shape=jax.ShapeDtypeStruct((2, 3, micro, band * side), bf),
        in_specs=[smem] + [hbm] * len(args),
        out_specs=vmem,
        scratch_shapes=[like(a) for a in args]
        + [
            pltpu.VMEM((8, near + px + near), f32),
            pltpu.VMEM(((band + 2) * side + 16, cb), f32),
            pltpu.VMEM((micro, (band + 2) * side, 3 * cb), bf),
            pltpu.SemaphoreType.DMA((len(args) + 2,)),
        ],
        compiler_params=pltpu.CompilerParams(vmem_limit_bytes=VMEM_ALL),
        cost_estimate=pl.CostEstimate(flops=4 * 10**9, bytes_accessed=7 * 10**6, transcendentals=10**6),
        name="base_section",
    )(steps, *args)


def last_kernel(ratio, tall, step_ref, *refs):
    hbm, out_ref = refs[: 11 + ratio], refs[11 + ratio]
    ids_ref, mine_ref, near_ref, far_ref, w_in_ref, gain_ref, head_ref, w_time_ref, conv_ref, query_ref, out_w_ref = refs[
        12 + ratio : 23 + ratio
    ]
    load, inbig, headbig, wpair, wq2, wo2, cond_pick, act, turn, *halves, sems = refs[23 + ratio :]
    slots = (halves[:3], halves[3:])
    seg, place = lax.axis_index("segment"), lax.axis_index("space")
    groups = lax.axis_size("space")
    micro = step_ref.shape[0]
    span = load.shape[1] - micro * LTXT
    pairs_io = [(hbm[4], w_in_ref), (hbm[5], gain_ref), (hbm[6], head_ref)]
    pairs_io += [(hbm[7 + n].at[1], ref) for n, ref in enumerate((w_time_ref, conv_ref, query_ref, out_w_ref))]
    pairs_io += [(hbm[0], ids_ref)]
    pairs_io += [(hbm[1 + n], ref) for n, ref in enumerate((mine_ref, near_ref, far_ref))]
    pairs_io += [(hbm[11 + k], load.at[k]) for k in range(ratio)]
    copies = begin(pairs_io, sems)
    chans = query_ref.shape[0]
    wide, high = mine_ref.shape[3:]
    ltxt = LTXT
    planes = 3 * wide
    phase = lax.rem(place, ratio)
    odd_place = lax.rem(place, 2) == 1
    cond_dev = high // tall
    pairs = wide // 2
    rows = high + 16
    lane2 = 2 * chans

    for copy in copies[:7]:
        copy.wait()
    bf = jnp.bfloat16
    sub = lax.broadcasted_iota(jnp.int32, (16, chans), 0)
    blank = jnp.zeros((16, chans), bf)
    spread_in = [jnp.broadcast_to(w_in_ref[c, 1:2].astype(jnp.float32), (16, chans)) for c in range(6)]
    spread_head = [jnp.broadcast_to(head_ref[c, 1:2].astype(jnp.float32), (16, chans)) for c in range(3)]
    for w in range(wide):
        lanes = slice(w * chans, (w + 1) * chans)
        here = sub == w % 16
        for rows_of, big in ((spread_in, inbig), (spread_head, headbig)):
            for c, row in enumerate(rows_of):
                one = jnp.where(here, row, 0.0).astype(bf)
                for n in range(wide // 16):
                    big[c * wide + 16 * n : c * wide + 16 * (n + 1), lanes] = one if n == w // 16 else blank
    zero_tap = jnp.zeros((chans, chans), jnp.bfloat16)
    for d in range(4):
        for a in range(3):
            at = (d * 3 + a) * chans
            wpair[at : at + chans, :chans] = conv_ref[3 * a + d] if d < 3 else zero_tap
            wpair[at : at + chans, chans:] = conv_ref[3 * a + d - 1] if d > 0 else zero_tap
    for dst, src in ((wq2, query_ref), (wo2, out_w_ref)):
        dst[:chans, :chans] = src[...]
        dst[:chans, chans:] = zero_tap
        dst[chans:, :chans] = zero_tap
        dst[chans:, chans:] = src[...]
    strip = cond_pick.shape[0] // 3
    pick_row = lax.broadcasted_iota(jnp.int32, (strip, planes), 0)
    pick_lane = lax.broadcasted_iota(jnp.int32, (strip, planes), 1)
    for c in range(3):
        hit = (pick_lane == c * wide + lax.rem(pick_row, wide))
        cond_pick[c * strip : (c + 1) * strip] = jnp.where(hit, 1.0, 0.0).astype(jnp.bfloat16)
    turn[...] = jnp.zeros_like(turn)
    for even, odd, _ in slots:
        even[0] = jnp.zeros(even.shape[1:], even.dtype)
        odd[pairs] = jnp.zeros(odd.shape[1:], odd.dtype)

    temb = fdot(embed(step_ref, 2, chans), w_time_ref[...])
    top_ok = jnp.where(place > 0, 1.0, 0.0)
    low_ok = jnp.where(place < groups - 1, 1.0, 0.0)
    gain0, gain1, gain2 = gain_ref[0, 1:2], gain_ref[1, 1:2], gain_ref[2, 1:2]
    inv = 1.0 / chans

    tile = lambda n: lax.div(lax.broadcasted_iota(jnp.int32, (lane2, lane2), n), chans)
    ones2 = jnp.where(tile(0) == tile(1), 1.0, 0.0).astype(jnp.bfloat16)
    gain0, gain1, gain2 = (jnp.concatenate([g, g], axis=1) for g in (gain0, gain1, gain2))

    def norm(x):
        total = fdot((x * x).astype(jnp.bfloat16), ones2)
        return x * lax.rsqrt(total * inv + 1e-06)

    tables = [levels(step_ref, m, 2) for m in range(micro)]
    for copy in copies[7:]:
        copy.wait()

    def lane_norm(x):
        return x * lax.rsqrt(jnp.sum(x * x, axis=-1, keepdims=True) * inv + 1e-06)

    duos = ratio // 2

    def spot(i):
        m, k = lax.div(i, ratio), lax.rem(i, ratio)
        duo = lax.rem(lax.div(phase, 2) - lax.rem(k, duos) + duos, duos)
        return m, k, 2 * duo + lax.rem(phase + lax.div(k, duos), 2)

    def front(i, slot):
        even, odd, hid = slots[slot]
        m, k, r = spot(i)
        temb_m = jnp.where(m == 0, temb[0:1], temb[1:2])
        temb2 = jnp.concatenate([temb_m, temb_m], axis=1)

        def window(ref, n):
            turn[n, :planes, :high] = ref[m, r].reshape(planes, high).astype(jnp.float32)
            return jnp.transpose(turn[n])

        body = window(mine_ref, 0)[:high, :planes]
        near = window(near_ref, 1)
        far = window(far_ref, 2)
        top = jnp.where(odd_place, near[high - 1 : high, :planes], far[high - 1 : high, :planes])
        low = jnp.where(odd_place, far[0:1, :planes], near[0:1, :planes])
        noise_rows = jnp.concatenate([body, top, low, jnp.zeros((14, planes), jnp.float32)], axis=0)
        blocks = [
            load[k, micro * ltxt + 16 * b : micro * ltxt + 16 * b + 8].astype(jnp.float32) for b in range(span // 16)
        ]
        band_planes = jnp.concatenate(blocks, axis=1)[:, :strip]
        row_h = lax.broadcasted_iota(jnp.int32, (rows, strip), 0)
        lane_px = lax.broadcasted_iota(jnp.int32, (rows, strip), 1)
        need = jnp.where(row_h < high, 1 + lax.div(row_h, tall), jnp.where(row_h == high, 0, cond_dev + 1))
        hit = lax.div(lane_px, wide) == need + phase * cond_dev
        spread = []
        for c in range(3):
            plane = jnp.where(m == 0, band_planes[2 * c : 2 * c + 1], band_planes[2 * c + 1 : 2 * c + 2])
            spread.append(jnp.where(hit, jnp.broadcast_to(plane, (rows, strip)), 0.0).astype(jnp.bfloat16))
        cond_rows = fdot(jnp.concatenate(spread, axis=1), cond_pick[...])
        pixels = jnp.concatenate([noise_rows, cond_rows], axis=1).astype(jnp.bfloat16)
        yield

        for t in range(pairs):
            h0 = fdot(pixels, inbig[:, t * lane2 : (t + 1) * lane2]) + temb2
            hid[t] = h0[:high]
            for par in range(2):
                x = silu(lane_norm(h0[:, par * chans : (par + 1) * chans]) * gain0[:, :chans])
                at = (t % 4) * 2 + par
                act[at, 8 : 8 + high] = x[:high]
                act[at, 7:8] = x[high : high + 1] * top_ok
                act[at, 8 + high : 9 + high] = x[high + 1 : high + 2] * low_ok
                wide3 = jnp.concatenate(
                    [act[at, 7 + a : 7 + a + high].astype(jnp.bfloat16) for a in range(3)], axis=1
                )
                if par == 0:
                    odd[t] = wide3
                else:
                    even[t + 1] = wide3
            if t % 2:
                yield

    subs = 2
    each = pairs // subs
    m_rows = each * high

    def back(i, slot):
        even, odd, hid = slots[slot]
        m, k, r = spot(i)
        keys = load[k, pl.ds(pl.multiple_of(m * ltxt, ltxt), ltxt), :chans]
        vals = load[k, pl.ds(pl.multiple_of(m * ltxt, ltxt), ltxt), chans:]
        kmask, vaug = pair_keys(keys, vals)
        bias = key_bias(ids_ref, m, seg * ratio + r)
        h1, mx = [], []
        for n in range(subs):
            at = n * each
            parts = (even[at : at + each], odd[at : at + each], even[at + 1 : at + 1 + each], odd[at + 1 : at + 1 + each])
            lhs = jnp.concatenate([part.reshape(m_rows, 3 * chans) for part in parts], axis=1)
            h1.append(fdot(lhs, wpair[...]) + hid[at : at + each].reshape(m_rows, lane2))
            yield
        query = []
        for n in range(subs):
            qn = fdot((norm(h1[n]) * gain1).astype(jnp.bfloat16), wq2[...])
            query.append((qn * (HD**-0.5 * LOG2E)).astype(jnp.bfloat16))
        yield
        for n in range(subs):
            mixed = []
            for p in range(2):
                mixed.append(attend_pair(query[n][:, p * chans : (p + 1) * chans], kmask, vaug, bias))
                yield
            mx.append(jnp.concatenate(mixed, axis=1))
        eps = jnp.zeros((planes, high), jnp.float32)
        for n in range(subs):
            h2 = h1[n] + fdot(mx[n], wo2[...])
            rows2 = (norm(h2) * gain2).astype(jnp.bfloat16).reshape(each, high, lane2)
            rows2 = jnp.concatenate([rows2[u] for u in range(each)], axis=1)
            eps = eps + lax.dot_general(
                headbig[:, n * each * lane2 : (n + 1) * each * lane2], rows2, NT, preferred_element_type=jnp.float32
            )
            yield
        noise = mine_ref[m, r].reshape(planes, high).astype(jnp.float32)
        ca, cb, cc, cd = (jnp.where(m == 0, tables[0][n], tables[1][n]) for n in range(4))
        clean = jnp.clip((noise - ca * eps) * cb, -1.0, 1.0)
        prior = cc * clean + cd * eps
        out_ref[0, m, r] = clean.astype(jnp.bfloat16).reshape(3, wide, high)
        out_ref[1, m, r] = prior.astype(jnp.bfloat16).reshape(3, wide, high)

    def together(*streams):
        live = list(streams)
        while live:
            live = [stream for stream in live if next(stream, stop) is not stop]

    stop = object()
    total = micro * ratio

    def couple(j, carry):
        together(back(2 * j, 0), front(2 * j + 1, 1))
        together(back(2 * j + 1, 1), front(2 * j + 2, 0))
        return carry

    together(front(0, 0))
    lax.fori_loop(0, total // 2 - 1, couple, 0)
    together(back(total - 2, 0), front(total - 1, 1))
    together(back(total - 1, 1))


def last_call(ratio, tall, steps, ids, noise, near, far, loads, weights):
    w_in, w_time, gains, w_conv, w_query, w_out, head = weights
    micro, _, _, wide, high = noise.shape
    chans = w_query.shape[1]
    planes = 3 * wide
    pairs = wide // 2
    strip = 512
    smem = pl.BlockSpec(memory_space=pltpu.SMEM)
    vmem = pl.BlockSpec(memory_space=pltpu.VMEM)
    hbm = pl.BlockSpec(memory_space=pltpu.HBM)
    bf, f32 = jnp.bfloat16, jnp.float32
    args = (ids, noise, near, far, w_in, gains, head, w_time, w_conv, w_query, w_out) + tuple(loads)
    part = pltpu.VMEM((micro, ratio, 3, wide, high), bf)
    return pl.pallas_call(
        functools.partial(last_kernel, ratio, tall),
        out_shape=jax.ShapeDtypeStruct((2, micro, ratio, 3, wide, high), bf),
        in_specs=[smem] + [hbm] * len(args),
        out_specs=vmem,
        scratch_shapes=[like(ids), part, part, part, like(w_in), like(gains), like(head)]
        + [like(a, 0) for a in (w_time, w_conv, w_query, w_out)]
        + [
            pltpu.VMEM((ratio,) + loads[0].shape, bf),
            pltpu.VMEM((2 * planes, wide * chans), bf),
            pltpu.VMEM((planes, wide * chans), bf),
            pltpu.VMEM((12 * chans, 2 * chans), bf),
            pltpu.VMEM((2 * chans, 2 * chans), bf),
            pltpu.VMEM((2 * chans, 2 * chans), bf),
            pltpu.VMEM((3 * strip, planes), bf),
            pltpu.VMEM((8, high + 16, chans), f32),
            pltpu.VMEM((3, 128, 128), f32),
        ]
        + [
            pltpu.VMEM((pairs + 1, high, 3 * chans), bf),
            pltpu.VMEM((pairs + 1, high, 3 * chans), bf),
            pltpu.VMEM((pairs, high, 2 * chans), f32),
        ]
        * 2
        + [
            pltpu.SemaphoreType.DMA((len(args),)),
        ],
        compiler_params=pltpu.CompilerParams(vmem_limit_bytes=VMEM_ALL),
        cost_estimate=pl.CostEstimate(flops=10**10, bytes_accessed=4 * 10**6, transcendentals=10**7),
        name="last_section",
    )(steps, *args)


def shards(
    text_states,
    token_ids,
    step_ids,
    base_noise,
    upscale_noise,
    final_noise,
    t5_gain,
    base_keyval,
    upscale_keyval,
    base_input,
    base_time,
    base_gain,
    base_conv,
    base_query,
    base_output,
    base_head,
    upscale_input,
    upscale_time,
    upscale_gain,
    upscale_conv,
    upscale_query,
    upscale_output,
    upscale_head,
):
    groups = lax.axis_size("space")
    segments = lax.axis_size("segment")
    ratio = groups // segments
    micro, _, ltxt, dt5 = text_states.shape
    rows_dev, cols = final_noise.shape[3:]
    tall = rows_dev * groups // cols

    noise_t = final_noise.swapaxes(3, 4)
    steps = step_ids.T
    chans_base = base_query.shape[1]
    base_x = base_noise.transpose(1, 2, 0, 3)[0]
    first_x = upscale_noise.transpose(1, 2, 0, 3)[0]
    base_w = (
        base_input,
        base_time,
        base_gain,
        base_conv.reshape(9 * chans_base, chans_base),
        base_query,
        base_output,
        base_head.T,
    )
    up_in = upscale_input.transpose(1, 0, 2)
    up_gain = upscale_gain.transpose(1, 0, 2)
    up_head = upscale_head.transpose(2, 0, 1)
    up_w = (up_in, upscale_time, up_gain, upscale_conv, upscale_query, upscale_output, up_head)
    kv_base, bundle, first_next, mine = front_call(
        segments,
        steps,
        token_ids,
        base_x,
        first_x,
        t5_gain[None],
        base_w,
        up_w,
        text_states.reshape(micro * ltxt, dt5),
        base_keyval,
        upscale_keyval,
        noise_t,
        ratio,
    )
    duos = ratio // 2
    cross = [
        [
            (s * groups + ratio * q + r, q * groups + ratio * s + 2 * ((r // 2 + k) % duos) + r % 2)
            for s in range(segments)
            for q in range(segments)
            for r in range(ratio)
        ]
        for k in range(duos)
    ]
    got = [lax.ppermute(bundle, ("segment", "space"), cross[k]) for k in range(duos)]
    swaps = [(i, i + 1) for i in range(0, groups - 1, 2)]
    near = lax.ppermute(mine, "space", swaps + [(j, i) for i, j in swaps])
    swaps = [(i, i + 1) for i in range(1, groups - 1, 2)]
    far = lax.ppermute(mine, "space", swaps + [(j, i) for i, j in swaps])

    early = base_call(segments, steps, token_ids, base_x, base_w, first_next, kv_base)
    mates = [(i, i ^ 1) for i in range(groups)]
    got, early = lax.optimization_barrier((got, early))
    loads = got + [lax.ppermute(array, "space", mates) for array in got]
    final = last_call(ratio, tall, steps, token_ids, mine, near, far, loads, up_w)
    early_states = early.transpose(0, 2, 1, 3)[:, :, None]
    return early_states, final.swapaxes(4, 5)


def solution(mesh):
    placed = (
        P(None, "space", None, None),
        P(),
        P(),
        P(None, "space", None, None),
        P(None, "space", None, None),
        P(None, None, None, "space", None),
    ) + (P(),) * 17

    return jax.shard_map(
        shards,
        mesh=mesh,
        in_specs=placed,
        out_specs=(
            P(None, None, "space", None, "segment"),
            P(None, None, "segment", None, "space", None),
        ),
        check_vma=False,
    )
```
